512 devices in a mesh: dp: 4 (over z_hi, core), ctx: 32 (over z_lo, y), tp: 4 (over x).
Axes of the slice: x: 4, y: 8, z: 8 (z_hi: 2, z_lo: 4; z = z_hi * 4 + z_lo), core: 2. Of those that a mesh axis runs over, the one named last changes fastest.
Arguments:
- q_feat: bfloat16 [32768, 4096], P(('dp', 'ctx'), 'tp'), parts along dimension 0, may hold values from -6 to 6
- k_feat: bfloat16 [32768, 4096], P(('dp', 'ctx'), 'tp'), parts along dimension 0, may hold values from -6 to 6
- v_feat: bfloat16 [32768, 4096], P(('dp', 'ctx'), 'tp'), parts along dimension 0, may hold values from -6 to 6
- short_taps: float32 [3, 3, 4096], P(None, None, 'tp'), may hold values from -3 to 3
- decay_rate: float32 [4096, 16], P('tp'), may hold values from 2.4414063e-05 to 0.04
- residue: float32 [4096, 16], P('tp'), may hold values from -4 to 4
- out_weight: bfloat16 [4096, 4096], P('tp', 'ctx'), may hold values from -0.8125 to 0.8125
- direction: float32 [4096], replicated, may hold values from -120 to 120
Outputs:
- ablated: bfloat16 [32768, 4096], P(('dp', 'ctx'), 'tp'), parts along dimension 0
- feature_level: float32 [32768], P(('dp', 'ctx')), parts along dimension 0
The draws below stay inside these ranges and needn't reach their ends.
There are 4 independent parts, one for each index of `dp`. The reference program is written for one: setup_inputs(seed, part) draws one part's arguments, and reference() takes and returns one part's arrays. A program takes and returns all parts, laid end to end along the dimension named above; an argument that names none is the same for every part. Nothing has to cross between parts.
All inputs are finite; a program needn't handle non-finite values.
Results may differ from the reference program's by a relative error of at most 0.019.
Values may be sent and summed in bfloat16 or wider, within the bound.
A program may use at most 128 MiB of HBM per device.

```python
import math
import jax
import jax.numpy as jnp
from jax import lax

C = 4096
DOUT = 4096
M = 16
K = 3
SEQ = 8192
N_TP = 4


def draw_decay_rate(key, part):
    lowest = 0.2 / SEQ
    highest = 0.04
    spread = jax.random.uniform(key, (C, M), jnp.float32)
    return lowest * (highest / lowest) ** spread


def shared_direction(key):
    value_key = jax.random.fold_in(key, 101)
    scale_key = jax.random.fold_in(key, 202)
    column = jnp.arange(DOUT, dtype=jnp.float32) / DOUT
    values = jax.random.truncated_normal(value_key, -4.0, 4.0, (DOUT,), jnp.float32)
    scales = jnp.exp(jax.random.uniform(scale_key, (DOUT,), jnp.float32) * math.log(10.0) + column * math.log(3.0))
    return values * scales


def draw_direction(key, part):
    return shared_direction(key)


def draw_out_weight(key, part):
    direction = shared_direction(key)
    base_key = jax.random.fold_in(key, 303)
    mix_key = jax.random.fold_in(key, 404)
    base_part = jax.random.truncated_normal(base_key, -4.0, 4.0, (C, DOUT), jnp.float32)
    mixing = jax.random.truncated_normal(mix_key, -4.0, 4.0, (C,), jnp.float32)
    return ((base_part + 0.1 * mixing[:, None] * direction[None, :]) / math.sqrt(C)).astype(jnp.bfloat16)


def block_scale(own_key, shape, cuts, smallest, largest):
    def one(dim, shards_of):
        heights = jax.random.uniform(jax.random.fold_in(jax.random.fold_in(own_key, 6), dim), (shards_of,), jnp.float32, smallest / len(cuts), largest / len(cuts))
        return jnp.repeat(jnp.exp(heights), shape[dim] // shards_of).reshape((-1,) + (1,) * (len(shape) - dim - 1))

    factor_of = one(*cuts[0])
    for cut in cuts[1:]:
        factor_of = factor_of * one(*cut)
    return factor_of


def normal_values(own_key, extent, scale, most, cuts=(), held_as=jnp.bfloat16):
    drawn = scale * jax.random.normal(own_key, extent, jnp.float32)
    if cuts:
        drawn = drawn * block_scale(own_key, extent, cuts, -0.22, 0.18)
    return jnp.clip(drawn, -most, most).astype(held_as)


def setup_inputs(seed: int = 0, part: int = 0) -> dict:
    splits = jax.random.split(jax.random.key(seed), 9)
    part_splits = jax.random.split(jax.random.fold_in(splits[8], part), 9)
    return {
        "q_feat": normal_values(part_splits[0], (SEQ, C), 1.0, 6.0, ((0, 32), (1, 4))),
        "k_feat": normal_values(part_splits[1], (SEQ, C), 1.0, 6.0, ((0, 32), (1, 4))),
        "v_feat": normal_values(part_splits[2], (SEQ, C), 1.0, 6.0, ((0, 32), (1, 4))),
        "short_taps": normal_values(splits[3], (3, K, C), 0.6, 3.0, ((2, 4),), jnp.float32),
        "decay_rate": draw_decay_rate(jax.random.fold_in(splits[8], 71), part),
        "residue": normal_values(splits[5], (C, M), 1.0, 4.0, ((0, 4),), jnp.float32),
        "out_weight": draw_out_weight(jax.random.fold_in(splits[8], 71), part),
        "direction": draw_direction(jax.random.fold_in(splits[8], 71), part),
    }


EPSILON = 1e-06

def short_filter(values, filter_taps):
    length = values.shape[0]
    padded = jnp.concatenate([jnp.zeros((K - 1, values.shape[1]), jnp.float32), values.astype(jnp.float32)], axis=0)
    summed = jnp.zeros((length, values.shape[1]), jnp.float32)
    for offset in range(K):
        summed = summed + filter_taps[offset][None, :] * padded[K - 1 - offset:K - 1 - offset + length]
    return summed

def long_filter(signal, decay_rate, gains):
    block_width = 128 if C % 128 == 0 else C
    block_count = C // block_width
    positions = jnp.arange(SEQ, dtype=jnp.float32)
    signal_blocks = signal.T.reshape(block_count, block_width, SEQ)
    rate_blocks = decay_rate.reshape(block_count, block_width, M)
    gain_blocks = gains.reshape(block_count, block_width, M)
    fft_length = 2 * SEQ

    def one_block(block_items):
        signal_block, rate_block, gain_block = block_items
        response = lax.optimization_barrier(jnp.sum(gain_block[:, :, None] * jnp.exp(-rate_block[:, :, None] * positions[None, None, :]), axis=1))
        product = jnp.fft.rfft(response, n=fft_length) * jnp.fft.rfft(signal_block, n=fft_length)
        return jnp.fft.irfft(product, n=fft_length)[:, :SEQ]
    result = lax.map(one_block, (signal_blocks, rate_blocks, gain_blocks))
    return result.reshape(C, SEQ).T

def reference(q_feat, k_feat, v_feat, short_taps, decay_rate, residue, out_weight, direction):
    query_short = short_filter(q_feat, short_taps[0])
    key_short = short_filter(k_feat, short_taps[1])
    value_short = short_filter(v_feat, short_taps[2])
    gains = residue * jnp.sqrt(-jnp.expm1(-2.0 * decay_rate)) * M ** (-0.5)
    mixed = long_filter(key_short * value_short, decay_rate, gains)
    gated = (query_short * mixed).astype(jnp.bfloat16)
    group_width = C // N_TP
    summed = jnp.zeros((SEQ, DOUT), jnp.float32)
    for group_index in range(N_TP):
        lower = group_index * group_width
        term_block = jnp.dot(gated[:, lower:lower + group_width], out_weight[lower:lower + group_width], preferred_element_type=jnp.float32)
        summed = summed + lax.optimization_barrier(term_block.astype(jnp.bfloat16)).astype(jnp.float32)
    norm_total = jnp.sum(direction * direction) + EPSILON
    feature_level = jnp.dot(summed, direction, precision=lax.Precision.HIGHEST) / norm_total
    ablated = (summed - feature_level[:, None] * direction[None, :]).astype(jnp.bfloat16)
    return (ablated, feature_level)
```

```python
import jax
import jax.numpy as jnp
from jax import lax
from jax.experimental import pallas as pl
from jax.experimental.pallas import tpu as pltpu
from jax.sharding import PartitionSpec as P

EPSILON = 1e-06
HIGHEST = lax.Precision.HIGHEST
MODES = 16
GROUPS = 8
TOKENS = 256
WIDTH = 1024
PITCH = TOKENS + 8
NY = 8
NZ = 4
NX = 4


def kernel(
    q_ref, k_ref, v_ref, taps_ref, rate_ref, gain_ref, w_ref, dir_ref,
    out_ref, level_ref,
    xq, xk, xv, qs, ys, gf, gb, state, decay, carry,
    halo_out, halo_in, st_out, st_in, tot_out, tot_in,
    wg, part_o, part_r, part_l, part_own, mid_r, mid_l, from_l, from_r,
    inner_acc, inner_out, inner_in,
    halo_sem, y_send, y_recv, z_send, z_recv, w_send, w_recv,
    s_send, s_recv, x_send, x_recv, i_send, i_recv,
):
    dp = lax.axis_index("dp")
    ctx = lax.axis_index("ctx")
    x = lax.axis_index("tp")
    z_hi = dp // 2
    core = dp % 2
    z = ctx // NY
    y = ctx % NY
    z_all = z_hi * NZ + z

    def at_y(d):
        return (dp, z * NY + (y + d) % NY, x)

    def at_z(d):
        return (dp, ((z + d) % NZ) * NY + y, x)

    def on_z_ring(d):
        other = (z_all + d + 2 * NZ) % (2 * NZ)
        return ((other // NZ) * 2 + core, (other % NZ) * NY + y, x)

    def at_x(d):
        return (dp, ctx, (x + d) % NX)

    sibling = (z_hi * 2 + 1 - core, ctx, x)
    after = (dp, (ctx + 1) % (NY * NZ), x)
    before = (dp, (ctx + NY * NZ - 1) % (NY * NZ), x)

    def remote(src, dst, send, recv, target):
        return pltpu.make_async_remote_copy(
            src_ref=src, dst_ref=dst, send_sem=send, recv_sem=recv,
            device_id=target, device_id_type=pl.DeviceIdType.MESH,
        )

    barrier = pltpu.get_barrier_semaphore()
    partners = (
        [at_y(d) for d in range(1, NY)]
        + [at_z(d) for d in range(1, NZ)]
        + [on_z_ring(1), on_z_ring(-1)]
        + [at_x(d) for d in range(1, NX)]
        + [sibling, after, before]
    )
    for target in partners:
        pl.semaphore_signal(
            barrier, inc=1, device_id=target, device_id_type=pl.DeviceIdType.MESH
        )
    wg[z, y, core] = w_ref[pl.ds(pl.multiple_of(core * 512, 512), 512), :]
    halo_out[0:2, :] = q_ref[TOKENS - 16:, :].astype(jnp.float32)[14:16, :]
    halo_out[2:4, :] = k_ref[TOKENS - 16:, :].astype(jnp.float32)[14:16, :]
    halo_out[4:6, :] = v_ref[TOKENS - 16:, :].astype(jnp.float32)[14:16, :]
    halo_out[6:8, :] = jnp.zeros((2, WIDTH), jnp.float32)
    pl.semaphore_wait(barrier, len(partners))

    def zz(d):
        return (z + d + NZ) % NZ

    def yy(d):
        return (y + d + NY) % NY

    lo, hi = pl.ds(0, 256), pl.ds(256, 256)
    sent = [
        [
            (z, y, 0), (z, y, 0),
            (zz(-1), y, 0, lo), (zz(1), y, 0, hi),
            (slice(None), y, 0), (slice(None), y, 0),
            (slice(None), yy(-1), 0), (slice(None), yy(1), 0),
            (slice(None), yy(-2), 0), (slice(None), yy(2), 0),
            (pl.ds(0, 2), yy(-3), 0), (pl.ds(2, 2), yy(3), 0),
        ],
        [
            (z, y, 1), (z, y, 1),
            (z, yy(-1), 1), (z, yy(1), 1),
            (z, yy(-2), 1), (z, yy(2), 1),
            (z, yy(-3), 1, lo), (z, yy(3), 1, hi),
            (z, slice(None), 1), (z, slice(None), 1),
            (zz(-1), pl.ds(0, 4), 1), (zz(1), pl.ds(4, 4), 1),
        ],
    ]
    got = [
        [
            (zz(-1), y, 0), (zz(1), y, 0),
            (zz(2), y, 0, lo), (zz(2), y, 0, hi),
            (slice(None), yy(-1), 0), (slice(None), yy(1), 0),
            (slice(None), yy(-2), 0), (slice(None), yy(2), 0),
            (slice(None), yy(-3), 0), (slice(None), yy(3), 0),
            (pl.ds(0, 2), yy(4), 0), (pl.ds(2, 2), yy(4), 0),
        ],
        [
            (z, yy(-1), 1), (z, yy(1), 1),
            (z, yy(-2), 1), (z, yy(2), 1),
            (z, yy(-3), 1), (z, yy(3), 1),
            (z, yy(4), 1, lo), (z, yy(4), 1, hi),
            (zz(-1), slice(None), 1), (zz(1), slice(None), 1),
            (zz(2), pl.ds(0, 4), 1), (zz(2), pl.ds(4, 4), 1),
        ],
    ]
    axis_of = [["z"] * 4 + ["y"] * 8, ["y"] * 8 + ["z"] * 4]
    to_sibling = [
        [(2, [(slice(None), y, 0)])]
        + [(3, got[0][4:6]), (4, got[0][6:8]), (5, got[0][8:10]), (6, got[0][10:12])],
        [(4, [(z, slice(None), 1)]), (5, got[1][8:10]), (6, got[1][10:12])],
    ]

    def ring(role, index, slot):
        sign = 1 if index % 2 == 0 else -1
        target = at_y(NY + sign) if axis_of[role][index] == "y" else on_z_ring(sign)
        region = wg.at[slot]
        return remote(region, region, w_send.at[index], w_recv.at[index], target)

    def handed(role, wanted=None):
        flat = []
        for step, slots in to_sibling[role]:
            for slot in slots:
                flat.append((step, slot))
        return [
            remote(wg.at[slot], wg.at[slot], s_send.at[i], s_recv.at[i], sibling)
            for i, (step, slot) in enumerate(flat)
            if wanted is None or step == wanted
        ]

    def weight_step(step):
        for role in range(2):
            @pl.when(core == role)
            def _(role=role):
                if step > 0:
                    for index in (2 * step - 2, 2 * step - 1):
                        ring(role, index, got[role][index]).wait_recv()
                if step < 6:
                    for index in (2 * step, 2 * step + 1):
                        ring(role, index, sent[role][index]).start()
                for copy in handed(role, step):
                    copy.start()

    def weight_end():
        for role in range(2):
            @pl.when(core == role)
            def _(role=role):
                for copy in handed(1 - role):
                    copy.wait_recv()

    def weight_drain():
        for role in range(2):
            @pl.when(core == role)
            def _(role=role):
                for index in range(12):
                    ring(role, index, sent[role][index]).wait_send()
                for copy in handed(role):
                    copy.wait_send()

    halo = remote(halo_out, halo_in, halo_sem.at[0], halo_sem.at[1], after)
    halo.start()
    weight_step(0)

    for ref, full in ((q_ref, xq), (k_ref, xk), (v_ref, xv)):
        for g in range(GROUPS):
            full[g * PITCH + 8:(g + 1) * PITCH, :] = (
                ref[:, g * 128:(g + 1) * 128].astype(jnp.float32)
            )
    state[...] = jnp.zeros_like(state)
    decay[...] = jnp.exp(-rate_ref[...])
    halo.wait_recv()
    for i, full in enumerate((xq, xk, xv)):
        for g in range(GROUPS):
            rows = halo_in[2 * i:2 * i + 2, g * 128:(g + 1) * 128]
            full[g * PITCH + 6:g * PITCH + 8, :] = jnp.where(ctx > 0, rows, 0.0)
    weight_step(1)

    def row(t):
        return pl.ds(t, GROUPS, stride=PITCH)

    def tile(ref, i):
        return ref[i * GROUPS:(i + 1) * GROUPS, :]

    def filter_step(i, _):
        start = i * 8
        short = []
        for f, full in enumerate((xq, xk, xv)):
            values = [full[row(start + 6 + j), :] for j in range(10)]
            taps = [tile(taps_ref, f * 3 + o) for o in range(3)]
            short.append([
                taps[0] * values[j + 2] + taps[1] * values[j + 1] + taps[2] * values[j]
                for j in range(8)
            ])
        for j in range(8):
            qs[start + j] = short[0][j]
        signal = [short[1][j] * short[2][j] for j in range(8)]
        total = [None] * 8
        for m in range(MODES):
            h = tile(state, m)
            a = tile(decay, m)
            c = tile(gain_ref, m)
            for j in range(8):
                h = a * h + signal[j]
                term = c * h
                total[j] = term if total[j] is None else total[j] + term
            state[m * GROUPS:(m + 1) * GROUPS, :] = h
        for j in range(8):
            ys[start + j] = total[j]
        return 0

    half = TOKENS // 16
    lax.fori_loop(0, half, filter_step, 0)
    weight_step(2)
    lax.fori_loop(half, 2 * half, filter_step, 0)

    st_out[...] = state[...].astype(jnp.bfloat16)
    y_copies = [
        remote(st_out, st_in.at[y], y_send.at[d], y_recv.at[d], at_y(d))
        for d in range(1, NY)
    ]
    for copy in y_copies:
        copy.start()
    st_in[y] = st_out[...]
    weight_step(3)
    block_decay = jnp.exp(-float(TOKENS) * rate_ref[...])
    for d in range(1, NY):
        remote(
            st_out, st_in.at[yy(-d)], y_send.at[d], y_recv.at[d], at_y(d)
        ).wait_recv()
    prefix = jnp.zeros((128, 128), jnp.float32)
    total = jnp.zeros((128, 128), jnp.float32)
    for other in range(NY):
        arrived = st_in[other].astype(jnp.float32)
        total = total * block_decay + arrived
        prefix = jnp.where(other < y, prefix * block_decay + arrived, prefix)
    tot_out[...] = total.astype(jnp.bfloat16)
    z_copies = [
        remote(tot_out, tot_in.at[z], z_send.at[d], z_recv.at[d], at_z(d))
        for d in range(1, NZ)
    ]
    for copy in z_copies:
        copy.start()
    tot_in[z] = tot_out[...]
    carry[...] = prefix
    weight_step(4)
    group_decay = jnp.exp(-float(TOKENS * NY) * rate_ref[...])
    own_decay = jnp.exp(-(TOKENS * y).astype(jnp.float32) * rate_ref[...])
    for d in range(1, NZ):
        remote(
            tot_out, tot_in.at[zz(-d)], z_send.at[d], z_recv.at[d], at_z(d)
        ).wait_recv()
    earlier = jnp.zeros((128, 128), jnp.float32)
    for other in range(NZ):
        arrived = tot_in[other].astype(jnp.float32)
        earlier = jnp.where(other < z, earlier * group_decay + arrived, earlier)
    carry[...] = gain_ref[...] * (carry[...] + own_decay * earlier)

    def carry_step(i, _):
        start = i * 8
        total = [ys[start + j] for j in range(8)]
        for m in range(MODES):
            h = tile(carry, m)
            a = tile(decay, m)
            for j in range(8):
                h = a * h
                total[j] = total[j] + h
            carry[m * GROUPS:(m + 1) * GROUPS, :] = h
        for j in range(8):
            gf[row(start + j), :] = qs[start + j] * total[j]
        return 0

    lax.fori_loop(0, 2 * half, carry_step, 0)
    weight_step(5)
    for g in range(GROUPS):
        gb[:, g * 128:(g + 1) * 128] = gf[
            g * PITCH:g * PITCH + TOKENS, :
        ].astype(jnp.bfloat16)
    inner_acc[...] = jnp.zeros_like(inner_acc)
    weight_step(6)
    weight_end()

    def project(d, part):
        target = (x + d) % NX

        def columns(n, _):
            pair = [
                wg[target, 2 * n + i].reshape(WIDTH, 128) for i in range(2)
            ]
            term = jnp.dot(
                gb[...], jnp.concatenate(pair, axis=1),
                preferred_element_type=jnp.float32,
            ).astype(jnp.bfloat16)
            part[:, pl.ds(pl.multiple_of(n * 256, 256), 256)] = term
            wide = term.astype(jnp.float32)
            at = target * NY + 2 * n
            inner_acc[...] += (
                wide[:, :128] * dir_ref[pl.ds(at, 1), :]
                + wide[:, 128:] * dir_ref[pl.ds(at + 1, 1), :]
            )
            return 0

        lax.fori_loop(0, 4, columns, 0)

    top, low = pl.ds(0, 128), pl.ds(128, 128)
    right, left = at_x(1), at_x(NX - 1)
    project(2, part_o)
    x_copies = [
        remote(part_o.at[top], mid_l, x_send.at[0], x_recv.at[0], right),
        remote(part_o.at[low], mid_r, x_send.at[1], x_recv.at[1], left),
        remote(part_r.at[low], from_l.at[low], x_send.at[2], x_recv.at[2], right),
        remote(part_l.at[top], from_r.at[top], x_send.at[3], x_recv.at[3], left),
        remote(part_r.at[top], from_l.at[top], x_send.at[4], x_recv.at[4], right),
        remote(part_l.at[low], from_r.at[low], x_send.at[5], x_recv.at[5], left),
    ]
    x_copies[0].start()
    x_copies[1].start()
    project(1, part_r)
    x_copies[2].start()
    project(3, part_l)
    x_copies[3].start()
    project(0, part_own)
    inner_out[...] = lax.dot_general(
        jnp.ones((8, 128), jnp.float32), inner_acc[...],
        (((1,), (1,)), ((), ())), precision=HIGHEST,
        preferred_element_type=jnp.float32,
    )
    i_copies = [
        remote(inner_out, inner_in.at[d], i_send.at[d], i_recv.at[d], at_x(d))
        for d in range(1, NX)
    ]
    for copy in i_copies:
        copy.start()
    x_copies[0].wait_recv()
    part_r[0:128, :] = (
        part_r[0:128, :].astype(jnp.float32) + mid_l[...].astype(jnp.float32)
    ).astype(jnp.bfloat16)
    x_copies[4].start()
    x_copies[1].wait_recv()
    part_l[128:256, :] = (
        part_l[128:256, :].astype(jnp.float32) + mid_r[...].astype(jnp.float32)
    ).astype(jnp.bfloat16)
    x_copies[5].start()

    for copy in i_copies:
        copy.wait_recv()
    norm_total = jnp.sum(dir_ref[...] * dir_ref[...]) + EPSILON
    level = (inner_out[...] + inner_in[1] + inner_in[2] + inner_in[3]) / norm_total
    level_ref[...] = level
    level_wide = jnp.transpose(jnp.broadcast_to(level[0:1, :], (128, TOKENS)))
    weight_drain()
    halo.wait_send()
    for copy in y_copies + z_copies + i_copies:
        copy.wait_send()
    for index in range(2, 6):
        x_copies[index].wait_recv()
    for n in range(NY):
        cols = slice(n * 128, (n + 1) * 128)
        summed = (
            part_own[:, cols].astype(jnp.float32)
            + from_l[:, cols].astype(jnp.float32)
            + from_r[:, cols].astype(jnp.float32)
        )
        out_ref[:, cols] = (
            summed - level_wide * dir_ref[pl.ds(x * NY + n, 1), :]
        ).astype(jnp.bfloat16)
    for copy in x_copies:
        copy.wait_send()


def shards(q_feat, k_feat, v_feat, short_taps, decay_rate, residue, out_weight, direction):
    gains = residue * jnp.sqrt(-jnp.expm1(-2.0 * decay_rate)) * MODES ** (-0.5)
    rate_rows = decay_rate.T.reshape(MODES * GROUPS, 128)
    gain_rows = gains.T.reshape(MODES * GROUPS, 128)
    taps_rows = short_taps.reshape(9 * GROUPS, 128)
    f32, bf16 = jnp.float32, jnp.bfloat16
    vmem = pltpu.VMEM
    dma = pltpu.SemaphoreType.DMA
    ablated, level = pl.pallas_call(
        kernel,
        out_shape=(
            jax.ShapeDtypeStruct((TOKENS, WIDTH), bf16),
            jax.ShapeDtypeStruct((8, TOKENS), f32),
        ),
        in_specs=[pl.BlockSpec(memory_space=pltpu.VMEM)] * 8,
        out_specs=(pl.BlockSpec(memory_space=pltpu.VMEM),) * 2,
        scratch_shapes=[
            vmem((GROUPS * PITCH, 128), f32),
            vmem((GROUPS * PITCH, 128), f32),
            vmem((GROUPS * PITCH, 128), f32),
            vmem((TOKENS, GROUPS, 128), f32),
            vmem((TOKENS, GROUPS, 128), f32),
            vmem((GROUPS * PITCH, 128), f32),
            vmem((TOKENS, WIDTH), bf16),
            vmem((128, 128), f32),
            vmem((128, 128), f32),
            vmem((128, 128), f32),
            vmem((8, WIDTH), f32),
            vmem((8, WIDTH), f32),
            vmem((128, 128), bf16),
            vmem((NY, 128, 128), bf16),
            vmem((128, 128), bf16),
            vmem((NZ, 128, 128), bf16),
            vmem((NZ, NY, 2, 512, 128), bf16),
            vmem((TOKENS, WIDTH), bf16),
            vmem((TOKENS, WIDTH), bf16),
            vmem((TOKENS, WIDTH), bf16),
            vmem((TOKENS, WIDTH), bf16),
            vmem((128, WIDTH), bf16),
            vmem((128, WIDTH), bf16),
            vmem((TOKENS, WIDTH), bf16),
            vmem((TOKENS, WIDTH), bf16),
            vmem((TOKENS, 128), f32),
            vmem((8, TOKENS), f32),
            vmem((NX, 8, TOKENS), f32),
            dma((2,)), dma((NY,)), dma((NY,)), dma((NZ,)), dma((NZ,)),
            dma((12,)), dma((12,)), dma((9,)), dma((9,)),
            dma((6,)), dma((6,)), dma((NX,)), dma((NX,)),
        ],
        compiler_params=pltpu.CompilerParams(
            collective_id=0, has_side_effects=True, vmem_limit_bytes=48 << 20
        ),
        name="mixing",
    )(
        q_feat, k_feat, v_feat, taps_rows, rate_rows, gain_rows, out_weight,
        direction.reshape(32, 128),
    )
    return ablated, level[0]


def solution(mesh):
    placed = (
        P(("dp", "ctx"), "tp"),
        P(("dp", "ctx"), "tp"),
        P(("dp", "ctx"), "tp"),
        P(None, None, "tp"),
        P("tp", None),
        P("tp", None),
        P("tp", "ctx"),
        P(),
    )
    return jax.shard_map(
        shards,
        mesh=mesh,
        in_specs=placed,
        out_specs=(P(("dp", "ctx"), "tp"), P(("dp", "ctx"))),
        check_vma=False,
    )
```

```python
import jax
import jax.numpy as jnp
from jax import lax
from jax.experimental import pallas as pl
from jax.experimental.pallas import tpu as pltpu
from jax.sharding import PartitionSpec as P

EPSILON = 1e-06
HIGHEST = lax.Precision.HIGHEST
MODES = 16
GROUPS = 8
TOKENS = 256
WIDTH = 1024
PITCH = TOKENS + 8
NY = 8
NZ = 4
NX = 4


def kernel(
    q_hbm, k_hbm, v_hbm, taps_hbm, rate_hbm, residue_hbm, w_hbm, dir_hbm,
    out_ref, level_ref,
    q_ref, k_ref, v_ref, taps_in, rate_in, residue_in, dir_ref,
    taps_ref, rate_ref, gain_ref,
    xq, xk, xv, qs, us, ys, gf, gb, state, decay, carry,
    halo_out, halo_in, st_out, st_in, tot_out, tot_in,
    wg, part_o, part_r, part_l, part_own, mid_r, mid_l, from_l, from_r,
    inner_acc, inner_out, inner_in,
    in_sem, halo_sem, y_send, y_recv, z_send, z_recv, w_send, w_recv,
    s_send, s_recv, x_send, x_recv, i_send, i_recv,
):
    dp = lax.axis_index("dp")
    ctx = lax.axis_index("ctx")
    x = lax.axis_index("tp")
    z_hi = dp // 2
    core = dp % 2
    z = ctx // NY
    y = ctx % NY
    z_all = z_hi * NZ + z

    def at_y(d):
        return (dp, z * NY + (y + d) % NY, x)

    def at_z(d):
        return (dp, ((z + d) % NZ) * NY + y, x)

    def on_z_ring(d):
        other = (z_all + d + 2 * NZ) % (2 * NZ)
        return ((other // NZ) * 2 + core, (other % NZ) * NY + y, x)

    def at_x(d):
        return (dp, ctx, (x + d) % NX)

    sibling = (z_hi * 2 + 1 - core, ctx, x)
    after = (dp, (ctx + 1) % (NY * NZ), x)
    before = (dp, (ctx + NY * NZ - 1) % (NY * NZ), x)

    def remote(src, dst, send, recv, target):
        return pltpu.make_async_remote_copy(
            src_ref=src, dst_ref=dst, send_sem=send, recv_sem=recv,
            device_id=target, device_id_type=pl.DeviceIdType.MESH,
        )

    barrier = pltpu.get_barrier_semaphore()
    partners = (
        [at_y(d) for d in range(1, NY)]
        + [at_z(d) for d in range(1, NZ)]
        + [on_z_ring(1), on_z_ring(-1)]
        + [at_x(d) for d in range(1, NX)]
        + [sibling, after, before]
    )
    for target in partners:
        pl.semaphore_signal(
            barrier, inc=1, device_id=target, device_id_type=pl.DeviceIdType.MESH
        )
    loads = [
        pltpu.make_async_copy(src, dst, in_sem.at[i])
        for i, (src, dst) in enumerate((
            (q_hbm, q_ref), (k_hbm, k_ref), (v_hbm, v_ref),
            (w_hbm.at[pl.ds(0, 512)], wg.at[z, y, 0]),
            (w_hbm.at[pl.ds(512, 512)], wg.at[z, y, 1]),
            (rate_hbm, rate_in), (residue_hbm, residue_in), (taps_hbm, taps_in),
            (dir_hbm, dir_ref),
        ))
    ]
    for load in loads:
        load.start()
    for load in loads:
        load.wait()
    halo_out[0:2, :] = q_ref[TOKENS - 16:, :].astype(jnp.float32)[14:16, :]
    halo_out[2:4, :] = k_ref[TOKENS - 16:, :].astype(jnp.float32)[14:16, :]
    halo_out[4:6, :] = v_ref[TOKENS - 16:, :].astype(jnp.float32)[14:16, :]
    halo_out[6:8, :] = jnp.zeros((2, WIDTH), jnp.float32)

    def zz(d):
        return (z + d + NZ) % NZ

    def yy(d):
        return (y + d + NY) % NY

    lo, hi = pl.ds(0, 256), pl.ds(256, 256)
    ring = [{}, {}]

    def piece(role, name, sign, axis, sent, got):
        ring[role][name] = (sign, axis, sent, got, len(ring[role]))

    near = (0, -1, 1, 2)
    last = {1: (0, -1), -1: (1, 2)}
    for sign in (1, -1):
        part = lo if sign > 0 else hi
        piece(0, ("z", sign, 1), sign, "z", (z, y, 0), (zz(-sign), y, 0))
        piece(0, ("z", sign, 2), sign, "z", (zz(-sign), y, 0, part), (zz(2), y, 0, part))
        for s in range(1, 5):
            for r in near if s < 4 else last[sign]:
                piece(
                    0, ("y", sign, s, r), sign, "y",
                    (zz(r), yy(-sign * (s - 1)), 0), (zz(r), yy(-sign * s), 0),
                )
        for s in range(1, 4):
            piece(
                1, ("y", sign, s), sign, "y",
                (z, yy(-sign * (s - 1)), 1), (z, yy(-sign * s), 1),
            )
        piece(
            1, ("y", sign, 4), sign, "y",
            (z, yy(-sign * 3), 1, part), (z, yy(4), 1, part),
        )
        for e in (0, -1, 1, -2, 2, -3, 3, 4):
            piece(1, ("z", sign, 1, e), sign, "z", (z, yy(e), 1), (zz(-sign), yy(e), 1))
            if (e >= 0 and e < 4) == (sign > 0):
                piece(1, ("z", sign, 2, e), sign, "z", (zz(-sign), yy(e), 1), (zz(2), yy(e), 1))

    handed = [[], []]

    def events_of_upper():
        def give(s, r, sign):
            return ("give", (zz(r), yy(-sign * s), 0))

        yield [("start", ("z", 1, 1)), ("start", ("z", -1, 1)),
               ("start", ("y", 1, 1, 0)), ("start", ("y", -1, 1, 0))]
        for sign in (1, -1):
            r = -sign
            yield [("wait", ("z", sign, 1)), ("start", ("z", sign, 2)),
                   ("start", ("y", 1, 1, r)), ("start", ("y", -1, 1, r)), give(0, r, 1)]
        for s in range(1, 5):
            if s == 2:
                pass
            for r in near:
                acts = []
                for sign in (1, -1):
                    if s == 4 and r not in last[sign]:
                        continue
                    acts.append(("wait", ("y", sign, s, r)))
                    if ("y", sign, s + 1, r) in ring[0]:
                        acts.append(("start", ("y", sign, s + 1, r)))
                    acts.append(give(s, r, sign))
                yield acts
                if s == 1 and r == 0:
                    yield [("wait", ("z", 1, 2)), ("wait", ("z", -1, 2)),
                           ("start", ("y", 1, 1, 2)), ("start", ("y", -1, 1, 2)),
                           give(0, 2, 1)]

    def events_of_lower():
        def both_z(e):
            return [("start", ("z", 1, 1, e)), ("start", ("z", -1, 1, e))]

        def z_near(e):
            acts = []
            for sign in (1, -1):
                acts.append(("wait", ("z", sign, 1, e)))
                if ("z", sign, 2, e) in ring[1]:
                    acts.append(("start", ("z", sign, 2, e)))
                acts.append(("give", (zz(-sign), yy(e), 1)))
            return acts

        def z_far(e):
            sign = 1 if ("z", 1, 2, e) in ring[1] else -1
            return [("wait", ("z", sign, 2, e)), ("give", (zz(2), yy(e), 1))]

        def y_near(s):
            acts = []
            for sign in (1, -1):
                e = -sign * s
                acts += [("wait", ("y", sign, s)), ("start", ("y", sign, s + 1))]
                acts += both_z(e) + [("give", (z, yy(e), 1))]
            return acts

        yield [("start", ("y", 1, 1)), ("start", ("y", -1, 1))] + both_z(0)
        yield y_near(1)
        yield z_near(0)
        yield y_near(2)
        yield z_near(-1)
        yield z_near(1) + z_far(0)
        yield y_near(3)
        yield z_near(-2) + z_far(-1)
        yield z_near(2) + z_far(1)
        yield ([("wait", ("y", 1, 4)), ("wait", ("y", -1, 4))] + both_z(4)
               + [("give", (z, yy(4), 1))])
        yield z_near(-3) + z_far(-2)
        yield z_near(3) + z_far(2)
        yield z_near(4)
        yield z_far(-3)
        yield z_far(3)
        yield z_far(4)

    events = [list(events_of_upper()), list(events_of_lower())]
    event_count = max(len(e) for e in events)
    for role in range(2):
        for acts in events[role]:
            for kind, what in acts:
                if kind == "give":
                    handed[role].append(what)
    done = [0]

    def ring_copy(role, name):
        sign, axis, sent, got, index = ring[role][name]
        target = at_y(NY + sign) if axis == "y" else on_z_ring(sign)
        return lambda slot: remote(
            wg.at[slot], wg.at[slot], w_send.at[index], w_recv.at[index], target
        )

    def give_copy(role, index):
        slot = wg.at[handed[role][index]]
        return remote(slot, slot, s_send.at[index], s_recv.at[index], sibling)

    given = [0, 0]

    def pump(count):
        first = done[0]
        done[0] = min(first + count, event_count)
        for role in range(2):
            @pl.when(core == role)
            def _(role=role):
                for acts in events[role][first:done[0]]:
                    for kind, what in acts:
                        if kind == "give":
                            give_copy(role, given[role]).start()
                            given[role] += 1
                        elif kind == "start":
                            ring_copy(role, what)(ring[role][what][2]).start()
                        else:
                            ring_copy(role, what)(ring[role][what][3]).wait_recv()

    def weight_end():
        pump(event_count)
        for role in range(2):
            @pl.when(core == role)
            def _(role=role):
                for index in range(len(handed[1 - role])):
                    give_copy(1 - role, index).wait_recv()

    def weight_drain():
        for role in range(2):
            @pl.when(core == role)
            def _(role=role):
                for name in ring[role]:
                    ring_copy(role, name)(ring[role][name][2]).wait_send()
                for index in range(len(handed[role])):
                    give_copy(role, index).wait_send()

    halo = remote(halo_out, halo_in, halo_sem.at[0], halo_sem.at[1], after)
    pl.semaphore_wait(barrier, len(partners))
    halo.start()
    pump(1)

    for g in range(GROUPS):
        cols = slice(g * 128, (g + 1) * 128)
        rate_ref[pl.ds(g, MODES, stride=GROUPS), :] = rate_in[:, cols]
        doubled = 2.0 * rate_in[:, cols]
        series = jnp.full_like(doubled, 1.0)
        for k in range(9, 1, -1):
            series = 1.0 - doubled * series * (1.0 / k)
        grown = jnp.where(doubled < 0.25, doubled * series, 1.0 - jnp.exp(-doubled))
        gain_ref[pl.ds(g, MODES, stride=GROUPS), :] = (
            residue_in[:, cols] * jnp.sqrt(grown) * MODES ** (-0.5)
        )
        for f in range(3):
            taps_ref[pl.ds(f * 3 * GROUPS + g, 3, stride=GROUPS), :] = taps_in[f, :, cols]
    for ref, full in ((q_ref, xq), (k_ref, xk), (v_ref, xv)):
        for g in range(GROUPS):
            full[g * PITCH + 8:(g + 1) * PITCH, :] = (
                ref[:, g * 128:(g + 1) * 128].astype(jnp.float32)
            )
    state[...] = jnp.zeros_like(state)
    decay[...] = jnp.exp(-rate_ref[...])

    def row(t):
        return pl.ds(t, GROUPS, stride=PITCH)

    def tile(ref, i):
        return ref[i * GROUPS:(i + 1) * GROUPS, :]

    def scan_block(i):
        start = i * 8
        short = []
        for f, full in enumerate((xq, xk, xv)):
            values = [full[row(start + 6 + j), :] for j in range(10)]
            taps = [tile(taps_ref, f * 3 + o) for o in range(3)]
            short.append([
                taps[0] * values[j + 2] + taps[1] * values[j + 1] + taps[2] * values[j]
                for j in range(8)
            ])
        signal = [short[1][j] * short[2][j] for j in range(8)]
        for j in range(8):
            qs[start + j] = short[0][j]
            us[start + j] = signal[j]
        return signal

    def state_step(i, _):
        signal = scan_block(i)
        for m in range(MODES):
            h = tile(state, m)
            a = tile(decay, m)
            for j in range(8):
                h = a * h + signal[j]
            state[m * GROUPS:(m + 1) * GROUPS, :] = h
        return 0

    def filter_step(i, _):
        start = i * 8
        signal = [us[start + j] for j in range(8)]
        total = [None] * 8
        for m in range(MODES):
            h = tile(carry, m)
            a = tile(decay, m)
            c = tile(gain_ref, m)
            for j in range(8):
                h = a * h + signal[j]
                term = c * h
                total[j] = term if total[j] is None else total[j] + term
            carry[m * GROUPS:(m + 1) * GROUPS, :] = h
        for j in range(8):
            ys[start + j] = total[j]
        return 0

    blocks = TOKENS // 8
    lax.fori_loop(1, blocks, state_step, 0)
    halo.wait_recv()
    for i, full in enumerate((xq, xk, xv)):
        for g in range(GROUPS):
            rows = halo_in[2 * i:2 * i + 2, g * 128:(g + 1) * 128]
            full[g * PITCH + 6:g * PITCH + 8, :] = jnp.where(ctx > 0, rows, 0.0)
    signal = scan_block(0)
    for m in range(MODES):
        a = tile(decay, m)
        h = signal[0]
        for j in range(1, 8):
            h = a * h + signal[j]
        rest = jnp.exp(-float(TOKENS - 8) * tile(rate_ref, m))
        state[m * GROUPS:(m + 1) * GROUPS, :] = tile(state, m) + rest * h

    st_out[...] = state[...].astype(jnp.bfloat16)
    y_copies = [
        remote(st_out, st_in.at[y], y_send.at[d], y_recv.at[d], at_y(d))
        for d in range(1, NY)
    ]
    for copy in y_copies:
        copy.start()
    st_in[y] = st_out[...]
    carry[...] = jnp.zeros_like(carry)
    for quarter in range(4):
        pump(1)
        lax.fori_loop(quarter * blocks // 4, (quarter + 1) * blocks // 4, filter_step, 0)
    pump(1)
    block_decay = jnp.exp(-float(TOKENS) * rate_ref[...])
    for d in range(1, NY):
        remote(
            st_out, st_in.at[yy(-d)], y_send.at[d], y_recv.at[d], at_y(d)
        ).wait_recv()
    prefix = jnp.zeros((128, 128), jnp.float32)
    total = jnp.zeros((128, 128), jnp.float32)
    for other in range(NY):
        arrived = st_in[other].astype(jnp.float32)
        total = total * block_decay + arrived
        prefix = jnp.where(other < y, prefix * block_decay + arrived, prefix)
    tot_out[...] = total.astype(jnp.bfloat16)
    z_copies = [
        remote(tot_out, tot_in.at[z], z_send.at[d], z_recv.at[d], at_z(d))
        for d in range(1, NZ)
    ]
    for copy in z_copies:
        copy.start()
    tot_in[z] = tot_out[...]
    carry[...] = prefix
    pump(2)
    group_decay = jnp.exp(-float(TOKENS * NY) * rate_ref[...])
    own_decay = jnp.exp(-(TOKENS * y).astype(jnp.float32) * rate_ref[...])
    for d in range(1, NZ):
        remote(
            tot_out, tot_in.at[zz(-d)], z_send.at[d], z_recv.at[d], at_z(d)
        ).wait_recv()
    earlier = jnp.zeros((128, 128), jnp.float32)
    for other in range(NZ):
        arrived = tot_in[other].astype(jnp.float32)
        earlier = jnp.where(other < z, earlier * group_decay + arrived, earlier)
    carry[...] = gain_ref[...] * (carry[...] + own_decay * earlier)

    def carry_step(i, _):
        start = i * 8
        total = [ys[start + j] for j in range(8)]
        for m in range(MODES):
            h = tile(carry, m)
            a = tile(decay, m)
            for j in range(8):
                h = a * h
                total[j] = total[j] + h
            carry[m * GROUPS:(m + 1) * GROUPS, :] = h
        for j in range(8):
            gf[row(start + j), :] = qs[start + j] * total[j]
        return 0

    pump(1)
    for quarter in range(4):
        lax.fori_loop(quarter * blocks // 4, (quarter + 1) * blocks // 4, carry_step, 0)
        pump(1)
    for g in range(GROUPS):
        gb[:, g * 128:(g + 1) * 128] = gf[
            g * PITCH:g * PITCH + TOKENS, :
        ].astype(jnp.bfloat16)
    inner_acc[...] = jnp.zeros_like(inner_acc)
    weight_end()

    def project(d, part):
        target = (x + d) % NX

        def columns(n, _):
            pair = [
                wg[target, 2 * n + i].reshape(WIDTH, 128) for i in range(2)
            ]
            term = jnp.dot(
                gb[...], jnp.concatenate(pair, axis=1),
                preferred_element_type=jnp.float32,
            ).astype(jnp.bfloat16)
            part[:, pl.ds(pl.multiple_of(n * 256, 256), 256)] = term
            wide = term.astype(jnp.float32)
            at = target * NY + 2 * n
            inner_acc[...] += (
                wide[:, :128] * dir_ref[pl.ds(at, 1), :]
                + wide[:, 128:] * dir_ref[pl.ds(at + 1, 1), :]
            )
            return 0

        lax.fori_loop(0, 4, columns, 0)

    top, low = pl.ds(0, 128), pl.ds(128, 128)
    right, left = at_x(1), at_x(NX - 1)
    project(2, part_o)
    x_copies = [
        remote(part_o.at[top], mid_l, x_send.at[0], x_recv.at[0], right),
        remote(part_o.at[low], mid_r, x_send.at[1], x_recv.at[1], left),
        remote(part_r.at[low], from_l.at[low], x_send.at[2], x_recv.at[2], right),
        remote(part_l.at[top], from_r.at[top], x_send.at[3], x_recv.at[3], left),
        remote(part_r.at[top], from_l.at[top], x_send.at[4], x_recv.at[4], right),
        remote(part_l.at[low], from_r.at[low], x_send.at[5], x_recv.at[5], left),
    ]
    x_copies[0].start()
    x_copies[1].start()
    project(1, part_r)
    x_copies[2].start()
    project(3, part_l)
    x_copies[3].start()
    project(0, part_own)
    inner_out[...] = lax.dot_general(
        jnp.ones((8, 128), jnp.float32), inner_acc[...],
        (((1,), (1,)), ((), ())), precision=HIGHEST,
        preferred_element_type=jnp.float32,
    )
    i_copies = [
        remote(inner_out, inner_in.at[d], i_send.at[d], i_recv.at[d], at_x(d))
        for d in range(1, NX)
    ]
    for copy in i_copies:
        copy.start()
    x_copies[0].wait_recv()
    part_r[0:128, :] = (
        part_r[0:128, :].astype(jnp.float32) + mid_l[...].astype(jnp.float32)
    ).astype(jnp.bfloat16)
    x_copies[4].start()
    x_copies[1].wait_recv()
    part_l[128:256, :] = (
        part_l[128:256, :].astype(jnp.float32) + mid_r[...].astype(jnp.float32)
    ).astype(jnp.bfloat16)
    x_copies[5].start()

    for copy in i_copies:
        copy.wait_recv()
    norm_total = jnp.sum(dir_ref[...] * dir_ref[...]) + EPSILON
    level = (inner_out[...] + inner_in[1] + inner_in[2] + inner_in[3]) / norm_total
    level_ref[...] = level[0:1, :]
    level_wide = jnp.transpose(jnp.broadcast_to(level[0:1, :], (128, TOKENS)))
    weight_drain()
    halo.wait_send()
    for copy in y_copies + z_copies + i_copies:
        copy.wait_send()
    for index in range(2, 6):
        x_copies[index].wait_recv()
    for n in range(NY):
        cols = slice(n * 128, (n + 1) * 128)
        summed = (
            part_own[:, cols].astype(jnp.float32)
            + from_l[:, cols].astype(jnp.float32)
            + from_r[:, cols].astype(jnp.float32)
        )
        out_ref[:, cols] = (
            summed - level_wide * dir_ref[pl.ds(x * NY + n, 1), :]
        ).astype(jnp.bfloat16)
    for copy in x_copies:
        copy.wait_send()


def shards(q_feat, k_feat, v_feat, short_taps, decay_rate, residue, out_weight, direction):
    f32, bf16 = jnp.float32, jnp.bfloat16
    vmem = pltpu.VMEM
    dma = pltpu.SemaphoreType.DMA
    ablated, level = pl.pallas_call(
        kernel,
        out_shape=(
            jax.ShapeDtypeStruct((TOKENS, WIDTH), bf16),
            jax.ShapeDtypeStruct((1, TOKENS), f32),
        ),
        in_specs=[pl.BlockSpec(memory_space=pltpu.HBM)] * 8,
        out_specs=(pl.BlockSpec(memory_space=pltpu.VMEM),) * 2,
        scratch_shapes=[
            vmem((TOKENS, WIDTH), bf16),
            vmem((TOKENS, WIDTH), bf16),
            vmem((TOKENS, WIDTH), bf16),
            vmem((3, 3, WIDTH), f32),
            vmem((MODES, WIDTH), f32),
            vmem((MODES, WIDTH), f32),
            vmem((32, 128), f32),
            vmem((9 * GROUPS, 128), f32),
            vmem((128, 128), f32),
            vmem((128, 128), f32),
            vmem((GROUPS * PITCH, 128), f32),
            vmem((GROUPS * PITCH, 128), f32),
            vmem((GROUPS * PITCH, 128), f32),
            vmem((TOKENS, GROUPS, 128), f32),
            vmem((TOKENS, GROUPS, 128), f32),
            vmem((TOKENS, GROUPS, 128), f32),
            vmem((GROUPS * PITCH, 128), f32),
            vmem((TOKENS, WIDTH), bf16),
            vmem((128, 128), f32),
            vmem((128, 128), f32),
            vmem((128, 128), f32),
            vmem((8, WIDTH), f32),
            vmem((8, WIDTH), f32),
            vmem((128, 128), bf16),
            vmem((NY, 128, 128), bf16),
            vmem((128, 128), bf16),
            vmem((NZ, 128, 128), bf16),
            vmem((NZ, NY, 2, 512, 128), bf16),
            vmem((TOKENS, WIDTH), bf16),
            vmem((TOKENS, WIDTH), bf16),
            vmem((TOKENS, WIDTH), bf16),
            vmem((TOKENS, WIDTH), bf16),
            vmem((128, WIDTH), bf16),
            vmem((128, WIDTH), bf16),
            vmem((TOKENS, WIDTH), bf16),
            vmem((TOKENS, WIDTH), bf16),
            vmem((TOKENS, 128), f32),
            vmem((8, TOKENS), f32),
            vmem((NX, 8, TOKENS), f32),
            dma((9,)), dma((2,)), dma((NY,)), dma((NY,)), dma((NZ,)), dma((NZ,)),
            dma((32,)), dma((32,)), dma((31,)), dma((31,)),
            dma((6,)), dma((6,)), dma((NX,)), dma((NX,)),
        ],
        compiler_params=pltpu.CompilerParams(
            collective_id=0, has_side_effects=True, vmem_limit_bytes=63 << 20
        ),
        name="mixing",
    )(
        q_feat, k_feat, v_feat, short_taps, decay_rate.T, residue.T, out_weight,
        direction.reshape(32, 128),
    )
    return ablated, level.reshape(TOKENS)


def solution(mesh):
    placed = (
        P(("dp", "ctx"), "tp"),
        P(("dp", "ctx"), "tp"),
        P(("dp", "ctx"), "tp"),
        P(None, None, "tp"),
        P("tp", None),
        P("tp", None),
        P("tp", "ctx"),
        P(),
    )
    return jax.shard_map(
        shards,
        mesh=mesh,
        in_specs=placed,
        out_specs=(P(("dp", "ctx"), "tp"), P(("dp", "ctx"))),
        check_vma=False,
    )
```

```python
import jax
import jax.numpy as jnp
from jax import lax
from jax.experimental import pallas as pl
from jax.experimental.pallas import tpu as pltpu
from jax.sharding import PartitionSpec as P

EPSILON = 1e-06
HIGHEST = lax.Precision.HIGHEST
MODES = 16
GROUPS = 8
TOKENS = 256
WIDTH = 1024
PITCH = TOKENS + 8
NY = 8
NZ = 4
NX = 4
UPPER = 384
LOWER = WIDTH - UPPER
COLUMN_GROUPS = ((0, -1, 1), (-2, 2), (-3, 3), (4,))
GROUP_START = (0, 384, 640, 896)


def kernel(
    q_hbm, k_hbm, v_hbm, taps_hbm, rate_hbm, residue_hbm, w_hbm, dir_hbm,
    out_ref, level_ref,
    q_ref, k_ref, v_ref, taps_in, rate_in, residue_in, dir_ref,
    taps_ref, rate_ref, gain_ref,
    xq, xk, xv, qs, us, ys, gf, gb, state, decay, carry,
    halo_out, halo_in, st_out, st_in, tot_out, tot_in,
    wg, part_o, part_r, part_l, part_own, mid_r, mid_l, from_l, from_r,
    inner_acc, inner_out, inner_in,
    in_sem, halo_sem, y_send, y_recv, z_send, z_recv, w_send, w_recv,
    s_send, s_recv, x_send, x_recv, i_send, i_recv,
):
    dp = lax.axis_index("dp")
    ctx = lax.axis_index("ctx")
    x = lax.axis_index("tp")
    z_hi = dp // 2
    core = dp % 2
    z = ctx // NY
    y = ctx % NY
    z_all = z_hi * NZ + z

    def at_y(d):
        return (dp, z * NY + (y + d) % NY, x)

    def at_z(d):
        return (dp, ((z + d) % NZ) * NY + y, x)

    def on_z_ring(d):
        other = (z_all + d + 2 * NZ) % (2 * NZ)
        return ((other // NZ) * 2 + core, (other % NZ) * NY + y, x)

    def at_x(d):
        return (dp, ctx, (x + d) % NX)

    sibling = (z_hi * 2 + 1 - core, ctx, x)
    after = (dp, (ctx + 1) % (NY * NZ), x)
    before = (dp, (ctx + NY * NZ - 1) % (NY * NZ), x)

    def remote(src, dst, send, recv, target):
        return pltpu.make_async_remote_copy(
            src_ref=src, dst_ref=dst, send_sem=send, recv_sem=recv,
            device_id=target, device_id_type=pl.DeviceIdType.MESH,
        )

    barrier = pltpu.get_barrier_semaphore()
    partners = (
        [at_y(d) for d in range(1, NY)]
        + [at_z(d) for d in range(1, NZ)]
        + [on_z_ring(1), on_z_ring(-1)]
        + [at_x(d) for d in range(1, NX)]
        + [sibling, after, before]
    )
    for target in partners:
        pl.semaphore_signal(
            barrier, inc=1, device_id=target, device_id_type=pl.DeviceIdType.MESH
        )
    loads = [
        pltpu.make_async_copy(src, dst, in_sem.at[i])
        for i, (src, dst) in enumerate((
            (q_hbm, q_ref), (k_hbm, k_ref), (v_hbm, v_ref),
            (w_hbm, wg.at[z, y]),
            (rate_hbm, rate_in), (residue_hbm, residue_in), (taps_hbm, taps_in),
            (dir_hbm, dir_ref),
        ))
    ]
    for load in loads:
        load.start()
    for load in loads:
        load.wait()
    halo_out[0:2, :] = q_ref[TOKENS - 16:, :].astype(jnp.float32)[14:16, :]
    halo_out[2:4, :] = k_ref[TOKENS - 16:, :].astype(jnp.float32)[14:16, :]
    halo_out[4:6, :] = v_ref[TOKENS - 16:, :].astype(jnp.float32)[14:16, :]
    halo_out[6:8, :] = jnp.zeros((2, WIDTH), jnp.float32)

    def zz(d):
        return (z + d + NZ) % NZ

    def yy(d):
        return (y + d + NY) % NY

    upper, lower = pl.ds(0, UPPER), pl.ds(UPPER, LOWER)
    upper_part = {1: pl.ds(0, UPPER // 2), -1: pl.ds(UPPER // 2, UPPER // 2)}
    lower_part = {1: pl.ds(UPPER, LOWER // 2), -1: pl.ds(UPPER + LOWER // 2, LOWER // 2)}
    ring = [{}, {}]

    def piece(role, name, sign, axis, sent, got):
        ring[role][name] = (sign, axis, sent, got, len(ring[role]))

    near = (0, -1, 1, 2)
    last = {1: (0, -1), -1: (1, 2)}
    for sign in (1, -1):
        half = upper_part[sign]
        piece(0, ("z", sign, 1), sign, "z", (z, y, upper), (zz(-sign), y, upper))
        piece(0, ("z", sign, 2), sign, "z", (zz(-sign), y, half), (zz(2), y, half))
        for s in range(1, 5):
            for r in near if s < 4 else last[sign]:
                piece(
                    0, ("y", sign, s, r), sign, "y",
                    (zz(r), yy(-sign * (s - 1)), upper), (zz(r), yy(-sign * s), upper),
                )
        for s in range(1, 4):
            piece(
                1, ("y", sign, s), sign, "y",
                (z, yy(-sign * (s - 1)), lower), (z, yy(-sign * s), lower),
            )
        half = lower_part[sign]
        piece(1, ("y", sign, 4), sign, "y", (z, yy(-sign * 3), half), (z, yy(4), half))
        for e in (0, -1, 1, -2, 2, -3, 3, 4):
            piece(
                1, ("z", sign, 1, e), sign, "z", (z, yy(e), lower), (zz(-sign), yy(e), lower)
            )
            if (e >= 0 and e < 4) == (sign > 0):
                piece(
                    1, ("z", sign, 2, e), sign, "z",
                    (zz(-sign), yy(e), lower), (zz(2), yy(e), lower),
                )

    handed = [[], []]

    def group_of(e):
        return max(abs(e) - 1, 0)

    def give(r, e, rows):
        return ("give", ((zz(r), yy(e), rows), group_of(e)))

    def events_of_upper():
        yield [("start", ("z", 1, 1)), ("start", ("z", -1, 1)), ]
        for sign in (1, -1):
            r = -sign
            yield [("wait", ("z", sign, 1)), ("start", ("z", sign, 2)),
                   give(r, 0, upper)]
        yield [("wait", ("z", 1, 2)), ("wait", ("z", -1, 2)), give(2, 0, upper)] + [
            ("start", ("y", sign, 1, r)) for r in near for sign in (1, -1)
        ]
        for s in range(1, 5):
            for r in near:
                acts = []
                for sign in (1, -1):
                    if s == 4 and r not in last[sign]:
                        continue
                    acts.append(("wait", ("y", sign, s, r)))
                    if ("y", sign, s + 1, r) in ring[0]:
                        acts.append(("start", ("y", sign, s + 1, r)))
                    acts.append(give(r, -sign * s, upper))
                yield acts

    def events_of_lower():
        def both_z(e):
            return [("start", ("z", 1, 1, e)), ("start", ("z", -1, 1, e))]

        def z_near(e):
            acts = []
            for sign in (1, -1):
                acts.append(("wait", ("z", sign, 1, e)))
                if ("z", sign, 2, e) in ring[1]:
                    acts.append(("start", ("z", sign, 2, e)))
                acts.append(give(-sign, e, lower))
            return acts

        def z_far(e):
            sign = 1 if ("z", 1, 2, e) in ring[1] else -1
            return [("wait", ("z", sign, 2, e)), give(2, e, lower)]

        def y_near(s):
            acts = []
            for sign in (1, -1):
                e = -sign * s
                acts += [("wait", ("y", sign, s)), ("start", ("y", sign, s + 1))]
                acts += both_z(e) + [give(0, e, lower)]
            return acts

        yield [("start", ("y", 1, 1)), ("start", ("y", -1, 1))] + both_z(0)
        yield y_near(1)
        yield z_near(0)
        yield y_near(2)
        yield z_near(-1)
        yield z_near(1) + z_far(0)
        yield y_near(3)
        yield z_near(-2) + z_far(-1)
        yield z_near(2) + z_far(1)
        yield ([("wait", ("y", 1, 4)), ("wait", ("y", -1, 4))] + both_z(4)
               + [give(0, 4, lower)])
        yield z_near(-3) + z_far(-2)
        yield z_near(3) + z_far(2)
        yield z_near(4) + z_far(-3)
        yield z_far(3)
        yield z_far(4)

    events = [list(events_of_upper()), list(events_of_lower())]
    for role in range(2):
        for acts in events[role]:
            for kind, what in acts:
                if kind == "give":
                    handed[role].append(what)

    def ring_copy(role, name):
        sign, axis, sent, got, index = ring[role][name]
        target = at_y(NY + sign) if axis == "y" else on_z_ring(sign)
        return lambda slot: remote(
            wg.at[slot], wg.at[slot], w_send.at[index], w_recv.at[index], target
        )

    def give_copy(role, index):
        slot = wg.at[handed[role][index][0]]
        return remote(slot, slot, s_send.at[index], s_recv.at[index], sibling)

    done = [0, 0]
    given = [0, 0]

    def pump_to(*counts):
        for role in range(2):
            first = done[role]
            done[role] = max(first, min(counts[role], len(events[role])))

            @pl.when(core == role)
            def _(role=role, first=first):
                for acts in events[role][first:done[role]]:
                    for kind, what in acts:
                        if kind == "give":
                            give_copy(role, given[role]).start()
                            given[role] += 1
                        elif kind == "start":
                            ring_copy(role, what)(ring[role][what][2]).start()
                        else:
                            ring_copy(role, what)(ring[role][what][3]).wait_recv()

    def weight_group(group):
        pump_to((8, 12, 16, 20)[group], (9, 12, 14, 15)[group])
        for role in range(2):
            @pl.when(core == role)
            def _(role=role):
                for index, (_slot, of) in enumerate(handed[1 - role]):
                    if of == group:
                        give_copy(1 - role, index).wait_recv()

    def weight_drain():
        for role in range(2):
            @pl.when(core == role)
            def _(role=role):
                for name in ring[role]:
                    ring_copy(role, name)(ring[role][name][2]).wait_send()
                for index in range(len(handed[role])):
                    give_copy(role, index).wait_send()

    halo = remote(halo_out, halo_in, halo_sem.at[0], halo_sem.at[1], after)
    pl.semaphore_wait(barrier, len(partners))
    halo.start()
    pump_to(1, 1)

    for g in range(GROUPS):
        cols = slice(g * 128, (g + 1) * 128)
        rate_ref[pl.ds(g, MODES, stride=GROUPS), :] = rate_in[:, cols]
        doubled = 2.0 * rate_in[:, cols]
        series = jnp.full_like(doubled, 1.0)
        for k in range(9, 1, -1):
            series = 1.0 - doubled * series * (1.0 / k)
        grown = jnp.where(doubled < 0.25, doubled * series, 1.0 - jnp.exp(-doubled))
        gain_ref[pl.ds(g, MODES, stride=GROUPS), :] = (
            residue_in[:, cols] * jnp.sqrt(grown) * MODES ** (-0.5)
        )
        for f in range(3):
            taps_ref[pl.ds(f * 3 * GROUPS + g, 3, stride=GROUPS), :] = taps_in[f, :, cols]
    for ref, full in ((q_ref, xq), (k_ref, xk), (v_ref, xv)):
        for g in range(GROUPS):
            full[g * PITCH + 8:(g + 1) * PITCH, :] = (
                ref[:, g * 128:(g + 1) * 128].astype(jnp.float32)
            )
    state[...] = jnp.zeros_like(state)
    decay[...] = jnp.exp(-rate_ref[...])

    def row(t):
        return pl.ds(t, GROUPS, stride=PITCH)

    def tile(ref, i):
        return ref[i * GROUPS:(i + 1) * GROUPS, :]

    def scan_block(i):
        start = i * 8
        short = []
        for f, full in enumerate((xq, xk, xv)):
            values = [full[row(start + 6 + j), :] for j in range(10)]
            taps = [tile(taps_ref, f * 3 + o) for o in range(3)]
            short.append([
                taps[0] * values[j + 2] + taps[1] * values[j + 1] + taps[2] * values[j]
                for j in range(8)
            ])
        signal = [short[1][j] * short[2][j] for j in range(8)]
        for j in range(8):
            qs[start + j] = short[0][j]
            us[start + j] = signal[j]
        return signal

    def state_step(i, _):
        signal = scan_block(i)
        for m in range(MODES):
            h = tile(state, m)
            a = tile(decay, m)
            for j in range(8):
                h = a * h + signal[j]
            state[m * GROUPS:(m + 1) * GROUPS, :] = h
        return 0

    def filter_step(i, _):
        start = i * 8
        signal = [us[start + j] for j in range(8)]
        total = [None] * 8
        for m in range(MODES):
            h = tile(carry, m)
            a = tile(decay, m)
            c = tile(gain_ref, m)
            for j in range(8):
                h = a * h + signal[j]
                term = c * h
                total[j] = term if total[j] is None else total[j] + term
            carry[m * GROUPS:(m + 1) * GROUPS, :] = h
        for j in range(8):
            ys[start + j] = total[j]
        return 0

    blocks = TOKENS // 8
    lax.fori_loop(1, blocks, state_step, 0)
    pump_to(3, 3)
    halo.wait_recv()
    for i, full in enumerate((xq, xk, xv)):
        for g in range(GROUPS):
            rows = halo_in[2 * i:2 * i + 2, g * 128:(g + 1) * 128]
            full[g * PITCH + 6:g * PITCH + 8, :] = jnp.where(ctx > 0, rows, 0.0)
    signal = scan_block(0)
    for m in range(MODES):
        a = tile(decay, m)
        h = signal[0]
        for j in range(1, 8):
            h = a * h + signal[j]
        rest = jnp.exp(-float(TOKENS - 8) * tile(rate_ref, m))
        state[m * GROUPS:(m + 1) * GROUPS, :] = tile(state, m) + rest * h

    st_out[...] = state[...].astype(jnp.bfloat16)
    y_copies = [
        remote(st_out, st_in.at[y], y_send.at[d], y_recv.at[d], at_y(d))
        for d in range(1, NY)
    ]
    for copy in y_copies:
        copy.start()
    st_in[y] = st_out[...]
    carry[...] = jnp.zeros_like(carry)
    pump_to(4, 3)
    for part in range(2):
        lax.fori_loop(part * blocks // 2, (part + 1) * blocks // 2, filter_step, 0)
        pump_to(4 + part, 4)
    pump_to(6, 5)
    block_decay = jnp.exp(-float(TOKENS) * rate_ref[...])
    for d in range(1, NY):
        remote(
            st_out, st_in.at[yy(-d)], y_send.at[d], y_recv.at[d], at_y(d)
        ).wait_recv()
    prefix = jnp.zeros((128, 128), jnp.float32)
    total = jnp.zeros((128, 128), jnp.float32)
    for other in range(NY):
        arrived = st_in[other].astype(jnp.float32)
        total = total * block_decay + arrived
        prefix = jnp.where(other < y, prefix * block_decay + arrived, prefix)
    tot_out[...] = total.astype(jnp.bfloat16)
    z_copies = [
        remote(tot_out, tot_in.at[z], z_send.at[d], z_recv.at[d], at_z(d))
        for d in range(1, NZ)
    ]
    for copy in z_copies:
        copy.start()
    tot_in[z] = tot_out[...]
    carry[...] = prefix
    pump_to(8, 6)
    group_decay = jnp.exp(-float(TOKENS * NY) * rate_ref[...])
    own_decay = jnp.exp(-(TOKENS * y).astype(jnp.float32) * rate_ref[...])
    for d in range(1, NZ):
        remote(
            tot_out, tot_in.at[zz(-d)], z_send.at[d], z_recv.at[d], at_z(d)
        ).wait_recv()
    earlier = jnp.zeros((128, 128), jnp.float32)
    for other in range(NZ):
        arrived = tot_in[other].astype(jnp.float32)
        earlier = jnp.where(other < z, earlier * group_decay + arrived, earlier)
    carry[...] = gain_ref[...] * (carry[...] + own_decay * earlier)

    def carry_step(i, _):
        start = i * 8
        total = [ys[start + j] for j in range(8)]
        for m in range(MODES):
            h = tile(carry, m)
            a = tile(decay, m)
            for j in range(8):
                h = a * h
                total[j] = total[j] + h
            carry[m * GROUPS:(m + 1) * GROUPS, :] = h
        for j in range(8):
            gf[row(start + j), :] = qs[start + j] * total[j]
        return 0

    lax.fori_loop(0, blocks, carry_step, 0)
    for g in range(GROUPS):
        gb[:, g * 128:(g + 1) * 128] = gf[
            g * PITCH:g * PITCH + TOKENS, :
        ].astype(jnp.bfloat16)
    inner_acc[...] = jnp.zeros_like(inner_acc)
    top, low = pl.ds(0, 128), pl.ds(128, 128)
    right, left = at_x(1), at_x(NX - 1)

    def span(group):
        return pl.ds(GROUP_START[group], 128 * len(COLUMN_GROUPS[group]))

    def project(d, part, group):
        target = (x + d) % NX
        at = [yy(e) for e in COLUMN_GROUPS[group]]
        blocks_here = [wg[target, c] for c in at]
        term = jnp.dot(
            gb[...],
            jnp.concatenate(blocks_here, axis=1) if len(at) > 1 else blocks_here[0],
            preferred_element_type=jnp.float32,
        ).astype(jnp.bfloat16)
        part[:, span(group)] = term
        wide = term.astype(jnp.float32)
        found = inner_acc[...]
        for i, c in enumerate(at):
            found += (
                wide[:, i * 128:(i + 1) * 128] * dir_ref[pl.ds(target * NY + c, 1), :]
            )
        inner_acc[...] = found

    def x_copy(group, index):
        cols = span(group)
        src, dst, target = (
            (part_o.at[top, cols], mid_l.at[:, cols], right),
            (part_o.at[low, cols], mid_r.at[:, cols], left),
            (part_r.at[low, cols], from_l.at[low, cols], right),
            (part_l.at[top, cols], from_r.at[top, cols], left),
            (part_r.at[top, cols], from_l.at[top, cols], right),
            (part_l.at[low, cols], from_r.at[low, cols], left),
        )[index]
        at = group * 6 + index
        return remote(src, dst, x_send.at[at], x_recv.at[at], target)

    def relay(group):
        cols = span(group)
        x_copy(group, 0).wait_recv()
        part_r[0:128, cols] = (
            part_r[0:128, cols].astype(jnp.float32) + mid_l[:, cols].astype(jnp.float32)
        ).astype(jnp.bfloat16)
        x_copy(group, 4).start()
        x_copy(group, 1).wait_recv()
        part_l[128:256, cols] = (
            part_l[128:256, cols].astype(jnp.float32) + mid_r[:, cols].astype(jnp.float32)
        ).astype(jnp.bfloat16)
        x_copy(group, 5).start()

    groups = len(COLUMN_GROUPS)
    pace = (
        ((10, 9), (11, 9), (12, 10), (12, 11)),
        ((13, 12), (13, 12), (14, 13), (15, 13)),
        ((16, 14), (17, 14), (18, 14), (18, 14)),
        ((20, 15),) * 4,
    )
    for group in range(groups):
        weight_group(group)
        project(2, part_o, group)
        x_copy(group, 0).start()
        x_copy(group, 1).start()
        pump_to(*pace[group][0])
        project(1, part_r, group)
        x_copy(group, 2).start()
        pump_to(*pace[group][1])
        project(3, part_l, group)
        x_copy(group, 3).start()
        if group in (1, 2):
            relay(group - 1)
        pump_to(*pace[group][2])
        project(0, part_own, group)
        pump_to(*pace[group][3])
        if group == 2:
            relay(group)
    inner_out[...] = lax.dot_general(
        jnp.ones((8, 128), jnp.float32), inner_acc[...],
        (((1,), (1,)), ((), ())), precision=HIGHEST,
        preferred_element_type=jnp.float32,
    )
    i_copies = [
        remote(inner_out, inner_in.at[d], i_send.at[d], i_recv.at[d], at_x(d))
        for d in range(1, NX)
    ]
    for copy in i_copies:
        copy.start()
    relay(groups - 1)
    for copy in i_copies:
        copy.wait_recv()
    norm_total = jnp.sum(dir_ref[...] * dir_ref[...]) + EPSILON
    level = (inner_out[...] + inner_in[1] + inner_in[2] + inner_in[3]) / norm_total
    level_ref[...] = level[0:1, :]
    level_wide = jnp.transpose(jnp.broadcast_to(level[0:1, :], (128, TOKENS)))
    weight_drain()
    halo.wait_send()
    for copy in y_copies + z_copies + i_copies:
        copy.wait_send()
    for group in range(groups):
        for index in range(2, 6):
            x_copy(group, index).wait_recv()
        for i, e in enumerate(COLUMN_GROUPS[group]):
            start = GROUP_START[group] + i * 128
            cols = slice(start, start + 128)
            summed = (
                part_own[:, cols].astype(jnp.float32)
                + from_l[:, cols].astype(jnp.float32)
                + from_r[:, cols].astype(jnp.float32)
            )
            at = yy(e)
            out_ref[:, pl.ds(pl.multiple_of(at * 128, 128), 128)] = (
                summed - level_wide * dir_ref[pl.ds(x * NY + at, 1), :]
            ).astype(jnp.bfloat16)
    for group in range(groups):
        for index in range(6):
            x_copy(group, index).wait_send()


def shards(q_feat, k_feat, v_feat, short_taps, decay_rate, residue, out_weight, direction):
    f32, bf16 = jnp.float32, jnp.bfloat16
    vmem = pltpu.VMEM
    dma = pltpu.SemaphoreType.DMA
    ablated, level = pl.pallas_call(
        kernel,
        out_shape=(
            jax.ShapeDtypeStruct((TOKENS, WIDTH), bf16),
            jax.ShapeDtypeStruct((1, TOKENS), f32),
        ),
        in_specs=[pl.BlockSpec(memory_space=pltpu.HBM)] * 8,
        out_specs=(pl.BlockSpec(memory_space=pltpu.VMEM),) * 2,
        scratch_shapes=[
            vmem((TOKENS, WIDTH), bf16),
            vmem((TOKENS, WIDTH), bf16),
            vmem((TOKENS, WIDTH), bf16),
            vmem((3, 3, WIDTH), f32),
            vmem((MODES, WIDTH), f32),
            vmem((MODES, WIDTH), f32),
            vmem((32, 128), f32),
            vmem((9 * GROUPS, 128), f32),
            vmem((128, 128), f32),
            vmem((128, 128), f32),
            vmem((GROUPS * PITCH, 128), f32),
            vmem((GROUPS * PITCH, 128), f32),
            vmem((GROUPS * PITCH, 128), f32),
            vmem((TOKENS, GROUPS, 128), f32),
            vmem((TOKENS, GROUPS, 128), f32),
            vmem((TOKENS, GROUPS, 128), f32),
            vmem((GROUPS * PITCH, 128), f32),
            vmem((TOKENS, WIDTH), bf16),
            vmem((128, 128), f32),
            vmem((128, 128), f32),
            vmem((128, 128), f32),
            vmem((8, WIDTH), f32),
            vmem((8, WIDTH), f32),
            vmem((128, 128), bf16),
            vmem((NY, 128, 128), bf16),
            vmem((128, 128), bf16),
            vmem((NZ, 128, 128), bf16),
            vmem((NZ, NY, WIDTH, 128), bf16),
            vmem((TOKENS, WIDTH), bf16),
            vmem((TOKENS, WIDTH), bf16),
            vmem((TOKENS, WIDTH), bf16),
            vmem((TOKENS, WIDTH), bf16),
            vmem((128, WIDTH), bf16),
            vmem((128, WIDTH), bf16),
            vmem((TOKENS, WIDTH), bf16),
            vmem((TOKENS, WIDTH), bf16),
            vmem((TOKENS, 128), f32),
            vmem((8, TOKENS), f32),
            vmem((NX, 8, TOKENS), f32),
            dma((8,)), dma((2,)), dma((NY,)), dma((NY,)), dma((NZ,)), dma((NZ,)),
            dma((32,)), dma((32,)), dma((31,)), dma((31,)),
            dma((24,)), dma((24,)), dma((NX,)), dma((NX,)),
        ],
        compiler_params=pltpu.CompilerParams(
            collective_id=0, has_side_effects=True, vmem_limit_bytes=63 << 20
        ),
        name="mixing",
    )(
        q_feat, k_feat, v_feat, short_taps, decay_rate.T, residue.T, out_weight,
        direction.reshape(32, 128),
    )
    return ablated, level.reshape(TOKENS)


def solution(mesh):
    placed = (
        P(("dp", "ctx"), "tp"),
        P(("dp", "ctx"), "tp"),
        P(("dp", "ctx"), "tp"),
        P(None, None, "tp"),
        P("tp", None),
        P("tp", None),
        P("tp", "ctx"),
        P(),
    )
    return jax.shard_map(
        shards,
        mesh=mesh,
        in_specs=placed,
        out_specs=(P(("dp", "ctx"), "tp"), P(("dp", "ctx"))),
        check_vma=False,
    )
```

```python
import jax
import jax.numpy as jnp
from jax import lax
from jax.experimental import pallas as pl
from jax.experimental.pallas import tpu as pltpu
from jax.sharding import PartitionSpec as P

EPSILON = 1e-06
HIGHEST = lax.Precision.HIGHEST
MODES = 16
GROUPS = 8
TOKENS = 256
WIDTH = 1024
PITCH = TOKENS + 8
NY = 8
NZ = 4
NX = 4
UPPER = 416
LOWER = WIDTH - UPPER
COLUMN_GROUPS = ((0, -1, 1), (-2, 2), (-3, 3), (4,))
GROUP_START = (0, 384, 640, 896)


def kernel(
    q_hbm, k_hbm, v_hbm, taps_hbm, rate_hbm, residue_hbm, w_hbm, dir_hbm,
    out_ref, level_ref,
    q_ref, k_ref, v_ref, taps_in, rate_in, residue_in, dir_ref,
    taps_ref, rate_ref, gain_ref,
    xq, xk, xv, qs, us, ys, gf, gb, state, decay, carry,
    halo_out, halo_in, st_out, st_in, tot_out, tot_in,
    wg, part_o, part_r, part_l, part_own, mid_r, mid_l, from_l, from_r,
    inner_acc, inner_out, inner_in,
    in_sem, halo_sem, y_send, y_recv, z_send, z_recv, w_send, w_recv,
    s_send, s_recv, x_send, x_recv, i_send, i_recv,
):
    dp = lax.axis_index("dp")
    ctx = lax.axis_index("ctx")
    x = lax.axis_index("tp")
    z_hi = dp // 2
    core = dp % 2
    z = ctx // NY
    y = ctx % NY
    z_all = z_hi * NZ + z

    def at_y(d):
        return (dp, z * NY + (y + d) % NY, x)

    def at_z(d):
        return (dp, ((z + d) % NZ) * NY + y, x)

    def on_z_ring(d):
        other = (z_all + d + 2 * NZ) % (2 * NZ)
        return ((other // NZ) * 2 + core, (other % NZ) * NY + y, x)

    def at_x(d):
        return (dp, ctx, (x + d) % NX)

    sibling = (z_hi * 2 + 1 - core, ctx, x)
    after = (dp, (ctx + 1) % (NY * NZ), x)
    before = (dp, (ctx + NY * NZ - 1) % (NY * NZ), x)

    def remote(src, dst, send, recv, target):
        return pltpu.make_async_remote_copy(
            src_ref=src, dst_ref=dst, send_sem=send, recv_sem=recv,
            device_id=target, device_id_type=pl.DeviceIdType.MESH,
        )

    barrier = pltpu.get_barrier_semaphore()
    partners = (
        [at_y(d) for d in range(1, NY)]
        + [at_z(d) for d in range(1, NZ)]
        + [on_z_ring(1), on_z_ring(-1)]
        + [at_x(d) for d in range(1, NX)]
        + [sibling, after, before]
    )
    for target in partners:
        pl.semaphore_signal(
            barrier, inc=1, device_id=target, device_id_type=pl.DeviceIdType.MESH
        )
    loads = [
        pltpu.make_async_copy(src, dst, in_sem.at[i])
        for i, (src, dst) in enumerate((
            (q_hbm, q_ref), (k_hbm, k_ref), (v_hbm, v_ref),
            (w_hbm, wg.at[z, y]),
            (rate_hbm, rate_in), (residue_hbm, residue_in), (taps_hbm, taps_in),
            (dir_hbm, dir_ref),
        ))
    ]
    for load in loads:
        load.start()
    for load in loads:
        load.wait()
    halo_out[0:2, :] = q_ref[TOKENS - 16:, :].astype(jnp.float32)[14:16, :]
    halo_out[2:4, :] = k_ref[TOKENS - 16:, :].astype(jnp.float32)[14:16, :]
    halo_out[4:6, :] = v_ref[TOKENS - 16:, :].astype(jnp.float32)[14:16, :]
    halo_out[6:8, :] = jnp.zeros((2, WIDTH), jnp.float32)

    def zz(d):
        return (z + d + NZ) % NZ

    def yy(d):
        return (y + d + NY) % NY

    upper, lower = pl.ds(0, UPPER), pl.ds(UPPER, LOWER)
    upper_part = {1: pl.ds(0, UPPER // 2), -1: pl.ds(UPPER // 2, UPPER // 2)}
    lower_sub = (pl.ds(UPPER, LOWER // 2), pl.ds(UPPER + LOWER // 2, LOWER // 2))
    ring = [{}, {}]

    def piece(role, name, sign, axis, sent, got):
        ring[role][name] = (sign, axis, sent, got, len(ring[role]))

    near = (0, -1, 1, 2)
    last = {1: (0, -1), -1: (1, 2)}
    for sign in (1, -1):
        half = upper_part[sign]
        piece(0, ("z", sign, 1), sign, "z", (z, y, upper), (zz(-sign), y, upper))
        piece(0, ("z", sign, 2), sign, "z", (zz(-sign), y, half), (zz(2), y, half))
        for s in range(1, 5):
            for r in near if s < 4 else last[sign]:
                piece(
                    0, ("y", sign, s, r), sign, "y",
                    (zz(r), yy(-sign * (s - 1)), upper), (zz(r), yy(-sign * s), upper),
                )
        for s in range(1, 4):
            for k in range(2):
                piece(
                    1, ("y", sign, s, k), sign, "y",
                    (z, yy(-sign * (s - 1)), lower_sub[k]), (z, yy(-sign * s), lower_sub[k]),
                )
        k = 0 if sign > 0 else 1
        piece(
            1, ("y", sign, 4, k), sign, "y",
            (z, yy(-sign * 3), lower_sub[k]), (z, yy(4), lower_sub[k]),
        )
        for e in (0, -1, 1, -2, 2, -3, 3, 4):
            for k in range(2):
                rows = lower_sub[k]
                piece(
                    1, ("z", sign, 1, e, k), sign, "z",
                    (z, yy(e), rows), (zz(-sign), yy(e), rows),
                )
                if (e >= 0 and e < 4) == (sign > 0):
                    piece(
                        1, ("z", sign, 2, e, k), sign, "z",
                        (zz(-sign), yy(e), rows), (zz(2), yy(e), rows),
                    )

    handed = [[], []]

    def group_of(e):
        return max(abs(e) - 1, 0)

    def give(r, e, rows):
        return ("give", ((zz(r), yy(e), rows), group_of(e)))

    def events_of_upper():
        yield [("start", ("z", 1, 1)), ("start", ("z", -1, 1)), ]
        for sign in (1, -1):
            r = -sign
            yield [("wait", ("z", sign, 1)), ("start", ("z", sign, 2)),
                   give(r, 0, upper)]
        yield [("wait", ("z", 1, 2)), ("wait", ("z", -1, 2)), give(2, 0, upper)] + [
            ("start", ("y", sign, 1, r)) for r in near for sign in (1, -1)
        ]
        for s in range(1, 5):
            for r in near:
                acts = []
                for sign in (1, -1):
                    if s == 4 and r not in last[sign]:
                        continue
                    acts.append(("wait", ("y", sign, s, r)))
                    if ("y", sign, s + 1, r) in ring[0]:
                        acts.append(("start", ("y", sign, s + 1, r)))
                    acts.append(give(r, -sign * s, upper))
                yield acts

    def events_of_lower():
        def both_z(e, k):
            return [("start", ("z", sign, 1, e, k)) for sign in (1, -1)]

        def z_near(e):
            acts = []
            for k in range(2):
                for sign in (1, -1):
                    acts.append(("wait", ("z", sign, 1, e, k)))
                    if ("z", sign, 2, e, k) in ring[1]:
                        acts.append(("start", ("z", sign, 2, e, k)))
            return acts + [give(-1, e, lower), give(1, e, lower)]

        def z_far(e):
            sign = 1 if ("z", 1, 2, e, 0) in ring[1] else -1
            return [("wait", ("z", sign, 2, e, k)) for k in range(2)] + [give(2, e, lower)]

        def y_near(s):
            acts = []
            for k in range(2):
                for sign in (1, -1):
                    acts.append(("wait", ("y", sign, s, k)))
                    if ("y", sign, s + 1, k) in ring[1]:
                        acts.append(("start", ("y", sign, s + 1, k)))
                for sign in (1, -1):
                    acts += both_z(-sign * s, k)
            return acts + [give(0, -s, lower), give(0, s, lower)]

        yield [
            ("start", ("y", sign, 1, k)) for k in range(2) for sign in (1, -1)
        ] + both_z(0, 0) + both_z(0, 1)
        yield y_near(1)
        yield z_near(0)
        yield y_near(2)
        yield z_near(-1)
        yield z_near(1) + z_far(0)
        yield y_near(3)
        yield z_near(-2) + z_far(-1)
        yield z_near(2) + z_far(1)
        yield ([("wait", ("y", 1, 4, 0))] + both_z(4, 0) + [("wait", ("y", -1, 4, 1))]
               + both_z(4, 1) + [give(0, 4, lower)])
        yield z_near(-3) + z_far(-2)
        yield z_near(3) + z_far(2)
        yield z_near(4) + z_far(-3)
        yield z_far(3)
        yield z_far(4)

    events = [list(events_of_upper()), list(events_of_lower())]
    for role in range(2):
        for acts in events[role]:
            for kind, what in acts:
                if kind == "give":
                    handed[role].append(what)

    def ring_copy(role, name):
        sign, axis, sent, got, index = ring[role][name]
        target = at_y(NY + sign) if axis == "y" else on_z_ring(sign)
        return lambda slot: remote(
            wg.at[slot], wg.at[slot], w_send.at[index], w_recv.at[index], target
        )

    def give_copy(role, index):
        slot = wg.at[handed[role][index][0]]
        return remote(slot, slot, s_send.at[index], s_recv.at[index], sibling)

    done = [0, 0]
    given = [0, 0]

    def pump_to(*counts):
        for role in range(2):
            first = done[role]
            done[role] = max(first, min(counts[role], len(events[role])))

            @pl.when(core == role)
            def _(role=role, first=first):
                for acts in events[role][first:done[role]]:
                    for kind, what in sorted(acts, key=lambda act: act[0] == "give"):
                        if kind == "give":
                            give_copy(role, given[role]).start()
                            given[role] += 1
                        elif kind == "start":
                            ring_copy(role, what)(ring[role][what][2]).start()
                        else:
                            ring_copy(role, what)(ring[role][what][3]).wait_recv()

    def weight_group(group):
        pump_to((8, 12, 16, 20)[group], (9, 12, 14, 15)[group])
        for role in range(2):
            @pl.when(core == role)
            def _(role=role):
                for index, (_slot, of) in enumerate(handed[1 - role]):
                    if of == group:
                        give_copy(1 - role, index).wait_recv()

    def weight_drain():
        for role in range(2):
            @pl.when(core == role)
            def _(role=role):
                for name in ring[role]:
                    ring_copy(role, name)(ring[role][name][2]).wait_send()
                for index in range(len(handed[role])):
                    give_copy(role, index).wait_send()

    halo = remote(halo_out, halo_in, halo_sem.at[0], halo_sem.at[1], after)
    pl.semaphore_wait(barrier, len(partners))
    halo.start()
    pump_to(1, 1)

    for g in range(GROUPS):
        cols = slice(g * 128, (g + 1) * 128)
        rate_ref[pl.ds(g, MODES, stride=GROUPS), :] = rate_in[:, cols]
        doubled = 2.0 * rate_in[:, cols]
        series = jnp.full_like(doubled, 1.0)
        for k in range(9, 1, -1):
            series = 1.0 - doubled * series * (1.0 / k)
        grown = jnp.where(doubled < 0.25, doubled * series, 1.0 - jnp.exp(-doubled))
        gain_ref[pl.ds(g, MODES, stride=GROUPS), :] = (
            residue_in[:, cols] * jnp.sqrt(grown) * MODES ** (-0.5)
        )
        for f in range(3):
            taps_ref[pl.ds(f * 3 * GROUPS + g, 3, stride=GROUPS), :] = taps_in[f, :, cols]
    for ref, full in ((q_ref, xq), (k_ref, xk), (v_ref, xv)):
        for g in range(GROUPS):
            full[g * PITCH + 8:(g + 1) * PITCH, :] = (
                ref[:, g * 128:(g + 1) * 128].astype(jnp.float32)
            )
    state[...] = jnp.zeros_like(state)
    decay[...] = jnp.exp(-rate_ref[...])

    def row(t):
        return pl.ds(t, GROUPS, stride=PITCH)

    def tile(ref, i):
        return ref[i * GROUPS:(i + 1) * GROUPS, :]

    def scan_block(i):
        start = i * 8
        short = []
        for f, full in enumerate((xq, xk, xv)):
            values = [full[row(start + 6 + j), :] for j in range(10)]
            taps = [tile(taps_ref, f * 3 + o) for o in range(3)]
            short.append([
                taps[0] * values[j + 2] + taps[1] * values[j + 1] + taps[2] * values[j]
                for j in range(8)
            ])
        signal = [short[1][j] * short[2][j] for j in range(8)]
        for j in range(8):
            qs[start + j] = short[0][j]
            us[start + j] = signal[j]
        return signal

    def state_step(i, _):
        signal = scan_block(i)
        for m in range(MODES):
            h = tile(state, m)
            a = tile(decay, m)
            for j in range(8):
                h = a * h + signal[j]
            state[m * GROUPS:(m + 1) * GROUPS, :] = h
        return 0

    def filter_step(i, _):
        start = i * 8
        signal = [us[start + j] for j in range(8)]
        total = [None] * 8
        for m in range(MODES):
            h = tile(carry, m)
            a = tile(decay, m)
            c = tile(gain_ref, m)
            for j in range(8):
                h = a * h + signal[j]
                term = c * h
                total[j] = term if total[j] is None else total[j] + term
            carry[m * GROUPS:(m + 1) * GROUPS, :] = h
        for j in range(8):
            ys[start + j] = total[j]
        return 0

    blocks = TOKENS // 8
    lax.fori_loop(1, blocks, state_step, 0)
    pump_to(3, 3)
    halo.wait_recv()
    for i, full in enumerate((xq, xk, xv)):
        for g in range(GROUPS):
            rows = halo_in[2 * i:2 * i + 2, g * 128:(g + 1) * 128]
            full[g * PITCH + 6:g * PITCH + 8, :] = jnp.where(ctx > 0, rows, 0.0)
    signal = scan_block(0)
    for m in range(MODES):
        a = tile(decay, m)
        h = signal[0]
        for j in range(1, 8):
            h = a * h + signal[j]
        rest = jnp.exp(-float(TOKENS - 8) * tile(rate_ref, m))
        state[m * GROUPS:(m + 1) * GROUPS, :] = tile(state, m) + rest * h

    st_out[...] = state[...].astype(jnp.bfloat16)
    y_copies = [
        remote(st_out, st_in.at[y], y_send.at[d], y_recv.at[d], at_y(d))
        for d in range(1, NY)
    ]
    for copy in y_copies:
        copy.start()
    st_in[y] = st_out[...]
    carry[...] = jnp.zeros_like(carry)
    pump_to(4, 3)
    for part, counts in enumerate(((4, 3), (4, 4), (5, 5), (6, 5))):
        lax.fori_loop(part * blocks // 4, (part + 1) * blocks // 4, filter_step, 0)
        pump_to(*counts)
    pump_to(7, 6)
    block_decay = jnp.exp(-float(TOKENS) * rate_ref[...])
    for d in range(1, NY):
        remote(
            st_out, st_in.at[yy(-d)], y_send.at[d], y_recv.at[d], at_y(d)
        ).wait_recv()
    prefix = jnp.zeros((128, 128), jnp.float32)
    total = jnp.zeros((128, 128), jnp.float32)
    for other in range(NY):
        arrived = st_in[other].astype(jnp.float32)
        total = total * block_decay + arrived
        prefix = jnp.where(other < y, prefix * block_decay + arrived, prefix)
    tot_out[...] = total.astype(jnp.bfloat16)
    z_copies = [
        remote(tot_out, tot_in.at[z], z_send.at[d], z_recv.at[d], at_z(d))
        for d in range(1, NZ)
    ]
    for copy in z_copies:
        copy.start()
    tot_in[z] = tot_out[...]
    carry[...] = prefix
    pump_to(8, 7)
    group_decay = jnp.exp(-float(TOKENS * NY) * rate_ref[...])
    own_decay = jnp.exp(-(TOKENS * y).astype(jnp.float32) * rate_ref[...])
    for d in range(1, NZ):
        remote(
            tot_out, tot_in.at[zz(-d)], z_send.at[d], z_recv.at[d], at_z(d)
        ).wait_recv()
    earlier = jnp.zeros((128, 128), jnp.float32)
    for other in range(NZ):
        arrived = tot_in[other].astype(jnp.float32)
        earlier = jnp.where(other < z, earlier * group_decay + arrived, earlier)
    carry[...] = gain_ref[...] * (carry[...] + own_decay * earlier)

    def carry_step(i, _):
        start = i * 8
        total = [ys[start + j] for j in range(8)]
        for m in range(MODES):
            h = tile(carry, m)
            a = tile(decay, m)
            for j in range(8):
                h = a * h
                total[j] = total[j] + h
            carry[m * GROUPS:(m + 1) * GROUPS, :] = h
        for j in range(8):
            gf[row(start + j), :] = qs[start + j] * total[j]
        return 0

    lax.fori_loop(0, blocks // 2, carry_step, 0)
    pump_to(9, 8)
    lax.fori_loop(blocks // 2, blocks, carry_step, 0)
    pump_to(11, 9)
    for g in range(GROUPS):
        gb[:, g * 128:(g + 1) * 128] = gf[
            g * PITCH:g * PITCH + TOKENS, :
        ].astype(jnp.bfloat16)
    inner_acc[...] = jnp.zeros_like(inner_acc)
    top, low = pl.ds(0, 128), pl.ds(128, 128)
    right, left = at_x(1), at_x(NX - 1)

    def span(group):
        return pl.ds(GROUP_START[group], 128 * len(COLUMN_GROUPS[group]))

    def project(d, part, group):
        target = (x + d) % NX
        at = [yy(e) for e in COLUMN_GROUPS[group]]
        blocks_here = [wg[target, c] for c in at]
        term = jnp.dot(
            gb[...],
            jnp.concatenate(blocks_here, axis=1) if len(at) > 1 else blocks_here[0],
            preferred_element_type=jnp.float32,
        ).astype(jnp.bfloat16)
        part[:, span(group)] = term
        wide = term.astype(jnp.float32)
        found = inner_acc[...]
        for i, c in enumerate(at):
            found += (
                wide[:, i * 128:(i + 1) * 128] * dir_ref[pl.ds(target * NY + c, 1), :]
            )
        inner_acc[...] = found

    def x_copy(group, index):
        cols = span(group)
        src, dst, target = (
            (part_o.at[top, cols], mid_l.at[:, cols], right),
            (part_o.at[low, cols], mid_r.at[:, cols], left),
            (part_r.at[low, cols], from_l.at[low, cols], right),
            (part_l.at[top, cols], from_r.at[top, cols], left),
            (part_r.at[top, cols], from_l.at[top, cols], right),
            (part_l.at[low, cols], from_r.at[low, cols], left),
        )[index]
        at = group * 6 + index
        return remote(src, dst, x_send.at[at], x_recv.at[at], target)

    def relay(group):
        cols = span(group)
        x_copy(group, 0).wait_recv()
        part_r[0:128, cols] = (
            part_r[0:128, cols].astype(jnp.float32) + mid_l[:, cols].astype(jnp.float32)
        ).astype(jnp.bfloat16)
        x_copy(group, 4).start()
        x_copy(group, 1).wait_recv()
        part_l[128:256, cols] = (
            part_l[128:256, cols].astype(jnp.float32) + mid_r[:, cols].astype(jnp.float32)
        ).astype(jnp.bfloat16)
        x_copy(group, 5).start()

    groups = len(COLUMN_GROUPS)
    pace = (
        ((10, 9), (11, 9), (12, 10), (12, 11)),
        ((13, 12), (13, 12), (14, 13), (15, 13)),
        ((16, 14), (17, 14), (18, 14), (18, 14)),
        ((20, 15),) * 4,
    )
    for group in range(groups):
        weight_group(group)
        project(2, part_o, group)
        x_copy(group, 0).start()
        x_copy(group, 1).start()
        pump_to(*pace[group][0])
        project(1, part_r, group)
        x_copy(group, 2).start()
        pump_to(*pace[group][1])
        project(3, part_l, group)
        x_copy(group, 3).start()
        if group in (1, 2):
            relay(group - 1)
        pump_to(*pace[group][2])
        project(0, part_own, group)
        pump_to(*pace[group][3])
        if group == 2:
            relay(group)
    inner_out[...] = lax.dot_general(
        jnp.ones((8, 128), jnp.float32), inner_acc[...],
        (((1,), (1,)), ((), ())), precision=HIGHEST,
        preferred_element_type=jnp.float32,
    )
    i_copies = [
        remote(inner_out, inner_in.at[d], i_send.at[d], i_recv.at[d], at_x(d))
        for d in range(1, NX)
    ]
    for copy in i_copies:
        copy.start()
    relay(groups - 1)
    for copy in i_copies:
        copy.wait_recv()
    norm_total = jnp.sum(dir_ref[...] * dir_ref[...]) + EPSILON
    level = (inner_out[...] + inner_in[1] + inner_in[2] + inner_in[3]) / norm_total
    level_ref[...] = level[0:1, :]
    level_wide = jnp.transpose(jnp.broadcast_to(level[0:1, :], (128, TOKENS)))
    weight_drain()
    halo.wait_send()
    for copy in y_copies + z_copies + i_copies:
        copy.wait_send()
    for group in range(groups):
        for index in range(2, 6):
            x_copy(group, index).wait_recv()
        for i, e in enumerate(COLUMN_GROUPS[group]):
            start = GROUP_START[group] + i * 128
            cols = slice(start, start + 128)
            summed = (
                part_own[:, cols].astype(jnp.float32)
                + from_l[:, cols].astype(jnp.float32)
                + from_r[:, cols].astype(jnp.float32)
            )
            at = yy(e)
            out_ref[:, pl.ds(pl.multiple_of(at * 128, 128), 128)] = (
                summed - level_wide * dir_ref[pl.ds(x * NY + at, 1), :]
            ).astype(jnp.bfloat16)
    for group in range(groups):
        for index in range(6):
            x_copy(group, index).wait_send()


def shards(q_feat, k_feat, v_feat, short_taps, decay_rate, residue, out_weight, direction):
    f32, bf16 = jnp.float32, jnp.bfloat16
    vmem = pltpu.VMEM
    dma = pltpu.SemaphoreType.DMA
    ablated, level = pl.pallas_call(
        kernel,
        out_shape=(
            jax.ShapeDtypeStruct((TOKENS, WIDTH), bf16),
            jax.ShapeDtypeStruct((1, TOKENS), f32),
        ),
        in_specs=[pl.BlockSpec(memory_space=pltpu.HBM)] * 8,
        out_specs=(pl.BlockSpec(memory_space=pltpu.VMEM),) * 2,
        scratch_shapes=[
            vmem((TOKENS, WIDTH), bf16),
            vmem((TOKENS, WIDTH), bf16),
            vmem((TOKENS, WIDTH), bf16),
            vmem((3, 3, WIDTH), f32),
            vmem((MODES, WIDTH), f32),
            vmem((MODES, WIDTH), f32),
            vmem((32, 128), f32),
            vmem((9 * GROUPS, 128), f32),
            vmem((128, 128), f32),
            vmem((128, 128), f32),
            vmem((GROUPS * PITCH, 128), f32),
            vmem((GROUPS * PITCH, 128), f32),
            vmem((GROUPS * PITCH, 128), f32),
            vmem((TOKENS, GROUPS, 128), f32),
            vmem((TOKENS, GROUPS, 128), f32),
            vmem((TOKENS, GROUPS, 128), f32),
            vmem((GROUPS * PITCH, 128), f32),
            vmem((TOKENS, WIDTH), bf16),
            vmem((128, 128), f32),
            vmem((128, 128), f32),
            vmem((128, 128), f32),
            vmem((8, WIDTH), f32),
            vmem((8, WIDTH), f32),
            vmem((128, 128), bf16),
            vmem((NY, 128, 128), bf16),
            vmem((128, 128), bf16),
            vmem((NZ, 128, 128), bf16),
            vmem((NZ, NY, WIDTH, 128), bf16),
            vmem((TOKENS, WIDTH), bf16),
            vmem((TOKENS, WIDTH), bf16),
            vmem((TOKENS, WIDTH), bf16),
            vmem((TOKENS, WIDTH), bf16),
            vmem((128, WIDTH), bf16),
            vmem((128, WIDTH), bf16),
            vmem((TOKENS, WIDTH), bf16),
            vmem((TOKENS, WIDTH), bf16),
            vmem((TOKENS, 128), f32),
            vmem((8, TOKENS), f32),
            vmem((NX, 8, TOKENS), f32),
            dma((8,)), dma((2,)), dma((NY,)), dma((NY,)), dma((NZ,)), dma((NZ,)),
            dma((62,)), dma((62,)), dma((31,)), dma((31,)),
            dma((24,)), dma((24,)), dma((NX,)), dma((NX,)),
        ],
        compiler_params=pltpu.CompilerParams(
            collective_id=0, has_side_effects=True, vmem_limit_bytes=63 << 20
        ),
        name="mixing",
    )(
        q_feat, k_feat, v_feat, short_taps, decay_rate.T, residue.T, out_weight,
        direction.reshape(32, 128),
    )
    return ablated, level.reshape(TOKENS)


def solution(mesh):
    placed = (
        P(("dp", "ctx"), "tp"),
        P(("dp", "ctx"), "tp"),
        P(("dp", "ctx"), "tp"),
        P(None, None, "tp"),
        P("tp", None),
        P("tp", None),
        P("tp", "ctx"),
        P(),
    )
    return jax.shard_map(
        shards,
        mesh=mesh,
        in_specs=placed,
        out_specs=(P(("dp", "ctx"), "tp"), P(("dp", "ctx"))),
        check_vma=False,
    )
```

```python
import jax
import jax.numpy as jnp
from jax import lax
from jax.experimental import pallas as pl
from jax.experimental.pallas import tpu as pltpu
from jax.sharding import PartitionSpec as P

EPSILON = 1e-06
HIGHEST = lax.Precision.HIGHEST
MODES = 16
GROUPS = 8
TOKENS = 256
WIDTH = 1024
PITCH = TOKENS + 8
NY = 8
NZ = 4
NX = 4
UPPER = 416
LOWER = WIDTH - UPPER
COLUMN_GROUPS = ((0, -1, 1), (-2, 2), (-3, 3), (4,))
GROUP_START = (0, 384, 640, 896)


def kernel(
    q_hbm, k_hbm, v_hbm, taps_hbm, rate_hbm, residue_hbm, w_hbm, dir_hbm,
    out_ref, level_ref,
    q_ref, k_ref, v_ref, taps_in, rate_in, residue_in, dir_ref,
    taps_ref, rate_ref, gain_ref,
    xq, xk, xv, qs, us, ys, gf, gb, state, decay, carry,
    halo_out, halo_in, st_out, st_in, tot_out, tot_in,
    wg, part_o, part_r, part_l, part_own, mid_r, mid_l, from_l, from_r,
    inner_acc, inner_out, inner_in,
    in_sem, halo_sem, y_send, y_recv, z_send, z_recv, w_send, w_recv,
    s_send, s_recv, x_send, x_recv, i_send, i_recv,
):
    dp = lax.axis_index("dp")
    ctx = lax.axis_index("ctx")
    x = lax.axis_index("tp")
    z_hi = dp // 2
    core = dp % 2
    z = ctx // NY
    y = ctx % NY
    z_all = z_hi * NZ + z

    def at_y(d):
        return (dp, z * NY + (y + d) % NY, x)

    def at_z(d):
        return (dp, ((z + d) % NZ) * NY + y, x)

    def on_z_ring(d):
        other = (z_all + d + 2 * NZ) % (2 * NZ)
        return ((other // NZ) * 2 + core, (other % NZ) * NY + y, x)

    def at_x(d):
        return (dp, ctx, (x + d) % NX)

    sibling = (z_hi * 2 + 1 - core, ctx, x)
    after = (dp, (ctx + 1) % (NY * NZ), x)
    before = (dp, (ctx + NY * NZ - 1) % (NY * NZ), x)

    def remote(src, dst, send, recv, target):
        return pltpu.make_async_remote_copy(
            src_ref=src, dst_ref=dst, send_sem=send, recv_sem=recv,
            device_id=target, device_id_type=pl.DeviceIdType.MESH,
        )

    loads = [
        pltpu.make_async_copy(src, dst, in_sem.at[i])
        for i, (src, dst) in enumerate((
            (w_hbm, wg.at[z, y]), (q_hbm, q_ref), (k_hbm, k_ref), (v_hbm, v_ref),
            (rate_hbm, rate_in), (residue_hbm, residue_in), (taps_hbm, taps_in),
            (dir_hbm, dir_ref),
        ))
    ]
    for load in loads:
        load.start()
    barrier = pltpu.get_barrier_semaphore()
    partners = (
        [at_y(d) for d in range(1, NY)]
        + [at_z(d) for d in range(1, NZ)]
        + [on_z_ring(1), on_z_ring(-1)]
        + [at_x(d) for d in range(1, NX)]
        + [sibling, after, before]
    )
    for target in partners:
        pl.semaphore_signal(
            barrier, inc=1, device_id=target, device_id_type=pl.DeviceIdType.MESH
        )
    def zz(d):
        return (z + d + NZ) % NZ

    def yy(d):
        return (y + d + NY) % NY

    upper, lower = pl.ds(0, UPPER), pl.ds(UPPER, LOWER)
    upper_part = {1: pl.ds(0, UPPER // 2), -1: pl.ds(UPPER // 2, UPPER // 2)}
    lower_sub = (pl.ds(UPPER, LOWER // 2), pl.ds(UPPER + LOWER // 2, LOWER // 2))
    ring = [{}, {}]

    def piece(role, name, sign, axis, sent, got):
        ring[role][name] = (sign, axis, sent, got, len(ring[role]))

    near = (0, -1, 1, 2)
    last = {1: (0, -1), -1: (1, 2)}
    for sign in (1, -1):
        half = upper_part[sign]
        piece(0, ("z", sign, 1), sign, "z", (z, y, upper), (zz(-sign), y, upper))
        piece(0, ("z", sign, 2), sign, "z", (zz(-sign), y, half), (zz(2), y, half))
        for s in range(1, 5):
            for r in near if s < 4 else last[sign]:
                piece(
                    0, ("y", sign, s, r), sign, "y",
                    (zz(r), yy(-sign * (s - 1)), upper), (zz(r), yy(-sign * s), upper),
                )
        for s in range(1, 4):
            for k in range(2):
                piece(
                    1, ("y", sign, s, k), sign, "y",
                    (z, yy(-sign * (s - 1)), lower_sub[k]), (z, yy(-sign * s), lower_sub[k]),
                )
        k = 0 if sign > 0 else 1
        piece(
            1, ("y", sign, 4, k), sign, "y",
            (z, yy(-sign * 3), lower_sub[k]), (z, yy(4), lower_sub[k]),
        )
        for e in (0, -1, 1, -2, 2, -3, 3, 4):
            for k in range(2):
                rows = lower_sub[k]
                piece(
                    1, ("z", sign, 1, e, k), sign, "z",
                    (z, yy(e), rows), (zz(-sign), yy(e), rows),
                )
                if (e >= 0 and e < 4) == (sign > 0):
                    piece(
                        1, ("z", sign, 2, e, k), sign, "z",
                        (zz(-sign), yy(e), rows), (zz(2), yy(e), rows),
                    )

    handed = [[], []]

    def group_of(e):
        return max(abs(e) - 1, 0)

    def give(r, e, rows):
        return ("give", ((zz(r), yy(e), rows), group_of(e)))

    def events_of_upper():
        yield [("start", ("z", 1, 1)), ("start", ("z", -1, 1)), ]
        for sign in (1, -1):
            r = -sign
            yield [("wait", ("z", sign, 1)), ("start", ("z", sign, 2)),
                   give(r, 0, upper)]
        yield [("wait", ("z", 1, 2)), ("wait", ("z", -1, 2)), give(2, 0, upper)] + [
            ("start", ("y", sign, 1, r)) for r in near for sign in (1, -1)
        ]
        for s in range(1, 5):
            for r in near:
                acts = []
                for sign in (1, -1):
                    if s == 4 and r not in last[sign]:
                        continue
                    acts.append(("wait", ("y", sign, s, r)))
                    if ("y", sign, s + 1, r) in ring[0]:
                        acts.append(("start", ("y", sign, s + 1, r)))
                    acts.append(give(r, -sign * s, upper))
                yield acts

    def events_of_lower():
        def both_z(e, k):
            return [("start", ("z", sign, 1, e, k)) for sign in (1, -1)]

        def z_near(e):
            acts = []
            for k in range(2):
                for sign in (1, -1):
                    acts.append(("wait", ("z", sign, 1, e, k)))
                    if ("z", sign, 2, e, k) in ring[1]:
                        acts.append(("start", ("z", sign, 2, e, k)))
            return acts + [give(-1, e, lower), give(1, e, lower)]

        def z_far(e):
            sign = 1 if ("z", 1, 2, e, 0) in ring[1] else -1
            return [("wait", ("z", sign, 2, e, k)) for k in range(2)] + [give(2, e, lower)]

        def y_near(s):
            acts = []
            for k in range(2):
                for sign in (1, -1):
                    acts.append(("wait", ("y", sign, s, k)))
                    if ("y", sign, s + 1, k) in ring[1]:
                        acts.append(("start", ("y", sign, s + 1, k)))
                for sign in (1, -1):
                    acts += both_z(-sign * s, k)
            return acts + [give(0, -s, lower), give(0, s, lower)]

        yield [
            ("start", ("y", sign, 1, k)) for k in range(2) for sign in (1, -1)
        ] + both_z(0, 0) + both_z(0, 1)
        yield y_near(1)
        yield z_near(0)
        yield y_near(2)
        yield z_near(-1)
        yield z_near(1) + z_far(0)
        yield y_near(3)
        yield z_near(-2) + z_far(-1)
        yield z_near(2) + z_far(1)
        yield ([("wait", ("y", 1, 4, 0))] + both_z(4, 0) + [("wait", ("y", -1, 4, 1))]
               + both_z(4, 1) + [give(0, 4, lower)])
        yield z_near(-3) + z_far(-2)
        yield z_near(3) + z_far(2)
        yield z_near(4) + z_far(-3)
        yield z_far(3)
        yield z_far(4)

    events = [list(events_of_upper()), list(events_of_lower())]
    for role in range(2):
        for acts in events[role]:
            for kind, what in acts:
                if kind == "give":
                    handed[role].append(what)

    def ring_copy(role, name):
        sign, axis, sent, got, index = ring[role][name]
        target = at_y(NY + sign) if axis == "y" else on_z_ring(sign)
        return lambda slot: remote(
            wg.at[slot], wg.at[slot], w_send.at[index], w_recv.at[index], target
        )

    def give_copy(role, index):
        slot = wg.at[handed[role][index][0]]
        return remote(slot, slot, s_send.at[index], s_recv.at[index], sibling)

    done = [0, 0]
    given = [0, 0]

    def pump_to(*counts):
        for role in range(2):
            first = done[role]
            done[role] = max(first, min(counts[role], len(events[role])))

            @pl.when(core == role)
            def _(role=role, first=first):
                for acts in events[role][first:done[role]]:
                    for kind, what in sorted(acts, key=lambda act: act[0] == "give"):
                        if kind == "give":
                            give_copy(role, given[role]).start()
                            given[role] += 1
                        elif kind == "start":
                            ring_copy(role, what)(ring[role][what][2]).start()
                        else:
                            ring_copy(role, what)(ring[role][what][3]).wait_recv()

    def weight_group(group):
        pump_to((8, 12, 16, 20)[group], (9, 12, 14, 15)[group])
        for role in range(2):
            @pl.when(core == role)
            def _(role=role):
                for index, (_slot, of) in enumerate(handed[1 - role]):
                    if of == group:
                        give_copy(1 - role, index).wait_recv()

    def weight_drain():
        for role in range(2):
            @pl.when(core == role)
            def _(role=role):
                for name in ring[role]:
                    ring_copy(role, name)(ring[role][name][2]).wait_send()
                for index in range(len(handed[role])):
                    give_copy(role, index).wait_send()

    halo = remote(halo_out, halo_in, halo_sem.at[0], halo_sem.at[1], after)
    loads[0].wait()
    pl.semaphore_wait(barrier, len(partners))
    pump_to(1, 1)
    for load in loads[1:]:
        load.wait()
    halo_out[0:2, :] = q_ref[TOKENS - 16:, :].astype(jnp.float32)[14:16, :]
    halo_out[2:4, :] = k_ref[TOKENS - 16:, :].astype(jnp.float32)[14:16, :]
    halo_out[4:6, :] = v_ref[TOKENS - 16:, :].astype(jnp.float32)[14:16, :]
    halo_out[6:8, :] = jnp.zeros((2, WIDTH), jnp.float32)
    halo.start()

    for g in range(GROUPS):
        cols = slice(g * 128, (g + 1) * 128)
        rate_ref[pl.ds(g, MODES, stride=GROUPS), :] = rate_in[:, cols]
        doubled = 2.0 * rate_in[:, cols]
        series = jnp.full_like(doubled, 1.0)
        for k in range(9, 1, -1):
            series = 1.0 - doubled * series * (1.0 / k)
        grown = jnp.where(doubled < 0.25, doubled * series, 1.0 - jnp.exp(-doubled))
        gain_ref[pl.ds(g, MODES, stride=GROUPS), :] = (
            residue_in[:, cols] * jnp.sqrt(grown) * MODES ** (-0.5)
        )
        for f in range(3):
            taps_ref[pl.ds(f * 3 * GROUPS + g, 3, stride=GROUPS), :] = taps_in[f, :, cols]
    for ref, full in ((q_ref, xq), (k_ref, xk), (v_ref, xv)):
        for g in range(GROUPS):
            full[g * PITCH + 8:(g + 1) * PITCH, :] = (
                ref[:, g * 128:(g + 1) * 128].astype(jnp.float32)
            )
    state[...] = jnp.zeros_like(state)
    decay[...] = jnp.exp(-rate_ref[...])

    def row(t):
        return pl.ds(t, GROUPS, stride=PITCH)

    def tile(ref, i):
        return ref[i * GROUPS:(i + 1) * GROUPS, :]

    def scan_block(i):
        start = i * 8
        short = []
        for f, full in enumerate((xq, xk, xv)):
            values = [full[row(start + 6 + j), :] for j in range(10)]
            taps = [tile(taps_ref, f * 3 + o) for o in range(3)]
            short.append([
                taps[0] * values[j + 2] + taps[1] * values[j + 1] + taps[2] * values[j]
                for j in range(8)
            ])
        signal = [short[1][j] * short[2][j] for j in range(8)]
        for j in range(8):
            qs[start + j] = short[0][j]
            us[start + j] = signal[j]
        return signal

    def state_step(i, _):
        signal = scan_block(i)
        for m in range(MODES):
            h = tile(state, m)
            a = tile(decay, m)
            for j in range(8):
                h = a * h + signal[j]
            state[m * GROUPS:(m + 1) * GROUPS, :] = h
        return 0

    def filter_step(i, _):
        start = i * 8
        signal = [us[start + j] for j in range(8)]
        total = [None] * 8
        for m in range(MODES):
            h = tile(carry, m)
            a = tile(decay, m)
            c = tile(gain_ref, m)
            for j in range(8):
                h = a * h + signal[j]
                term = c * h
                total[j] = term if total[j] is None else total[j] + term
            carry[m * GROUPS:(m + 1) * GROUPS, :] = h
        for j in range(8):
            ys[start + j] = total[j]
        return 0

    blocks = TOKENS // 8
    lax.fori_loop(1, blocks, state_step, 0)
    pump_to(3, 3)
    halo.wait_recv()
    for i, full in enumerate((xq, xk, xv)):
        for g in range(GROUPS):
            rows = halo_in[2 * i:2 * i + 2, g * 128:(g + 1) * 128]
            full[g * PITCH + 6:g * PITCH + 8, :] = jnp.where(ctx > 0, rows, 0.0)
    signal = scan_block(0)
    for m in range(MODES):
        a = tile(decay, m)
        h = signal[0]
        for j in range(1, 8):
            h = a * h + signal[j]
        rest = jnp.exp(-float(TOKENS - 8) * tile(rate_ref, m))
        state[m * GROUPS:(m + 1) * GROUPS, :] = tile(state, m) + rest * h

    st_out[...] = state[...].astype(jnp.bfloat16)
    y_copies = [
        remote(st_out, st_in.at[y], y_send.at[d], y_recv.at[d], at_y(d))
        for d in range(1, NY)
    ]
    for d in (4, 3, 5, 2, 6, 1, 7):
        y_copies[d - 1].start()
    st_in[y] = st_out[...]
    carry[...] = jnp.zeros_like(carry)
    pump_to(4, 3)
    for part, counts in enumerate(((4, 3), (4, 4), (5, 5), (6, 5))):
        lax.fori_loop(part * blocks // 4, (part + 1) * blocks // 4, filter_step, 0)
        pump_to(*counts)
    pump_to(7, 6)
    block_decay = jnp.exp(-float(TOKENS) * rate_ref[...])
    for d in range(1, NY):
        remote(
            st_out, st_in.at[yy(-d)], y_send.at[d], y_recv.at[d], at_y(d)
        ).wait_recv()
    prefix = jnp.zeros((128, 128), jnp.float32)
    total = jnp.zeros((128, 128), jnp.float32)
    for other in range(NY):
        arrived = st_in[other].astype(jnp.float32)
        total = total * block_decay + arrived
        prefix = jnp.where(other < y, prefix * block_decay + arrived, prefix)
    tot_out[...] = total.astype(jnp.bfloat16)
    z_copies = [
        remote(tot_out, tot_in.at[z], z_send.at[d], z_recv.at[d], at_z(d))
        for d in range(1, NZ)
    ]
    for copy in z_copies:
        copy.start()
    tot_in[z] = tot_out[...]
    carry[...] = prefix
    pump_to(8, 7)
    group_decay = jnp.exp(-float(TOKENS * NY) * rate_ref[...])
    own_decay = jnp.exp(-(TOKENS * y).astype(jnp.float32) * rate_ref[...])
    for d in range(1, NZ):
        remote(
            tot_out, tot_in.at[zz(-d)], z_send.at[d], z_recv.at[d], at_z(d)
        ).wait_recv()
    earlier = jnp.zeros((128, 128), jnp.float32)
    for other in range(NZ):
        arrived = tot_in[other].astype(jnp.float32)
        earlier = jnp.where(other < z, earlier * group_decay + arrived, earlier)
    carry[...] = gain_ref[...] * (carry[...] + own_decay * earlier)

    def carry_step(i, _):
        start = i * 8
        total = [ys[start + j] for j in range(8)]
        for m in range(MODES):
            h = tile(carry, m)
            a = tile(decay, m)
            for j in range(8):
                h = a * h
                total[j] = total[j] + h
            carry[m * GROUPS:(m + 1) * GROUPS, :] = h
        for j in range(8):
            gf[row(start + j), :] = qs[start + j] * total[j]
        return 0

    lax.fori_loop(0, blocks // 2, carry_step, 0)
    pump_to(9, 8)
    lax.fori_loop(blocks // 2, blocks, carry_step, 0)
    pump_to(11, 9)
    for g in range(GROUPS):
        gb[:, g * 128:(g + 1) * 128] = gf[
            g * PITCH:g * PITCH + TOKENS, :
        ].astype(jnp.bfloat16)
    inner_acc[...] = jnp.zeros_like(inner_acc)
    top, low = pl.ds(0, 128), pl.ds(128, 128)
    right, left = at_x(1), at_x(NX - 1)

    def span(group):
        return pl.ds(GROUP_START[group], 128 * len(COLUMN_GROUPS[group]))

    def project(d, part, group):
        target = (x + d) % NX
        at = [yy(e) for e in COLUMN_GROUPS[group]]
        blocks_here = [wg[target, c] for c in at]
        term = jnp.dot(
            gb[...],
            jnp.concatenate(blocks_here, axis=1) if len(at) > 1 else blocks_here[0],
            preferred_element_type=jnp.float32,
        ).astype(jnp.bfloat16)
        part[:, span(group)] = term
        wide = term.astype(jnp.float32)
        found = inner_acc[...]
        for i, c in enumerate(at):
            found += (
                wide[:, i * 128:(i + 1) * 128] * dir_ref[pl.ds(target * NY + c, 1), :]
            )
        inner_acc[...] = found

    def x_copy(group, index):
        cols = span(group)
        src, dst, target = (
            (part_o.at[top, cols], mid_l.at[:, cols], right),
            (part_o.at[low, cols], mid_r.at[:, cols], left),
            (part_r.at[low, cols], from_l.at[low, cols], right),
            (part_l.at[top, cols], from_r.at[top, cols], left),
            (part_r.at[top, cols], from_l.at[top, cols], right),
            (part_l.at[low, cols], from_r.at[low, cols], left),
        )[index]
        at = group * 6 + index
        return remote(src, dst, x_send.at[at], x_recv.at[at], target)

    def relay(group):
        cols = span(group)
        x_copy(group, 0).wait_recv()
        part_r[0:128, cols] = (
            part_r[0:128, cols].astype(jnp.float32) + mid_l[:, cols].astype(jnp.float32)
        ).astype(jnp.bfloat16)
        x_copy(group, 4).start()
        x_copy(group, 1).wait_recv()
        part_l[128:256, cols] = (
            part_l[128:256, cols].astype(jnp.float32) + mid_r[:, cols].astype(jnp.float32)
        ).astype(jnp.bfloat16)
        x_copy(group, 5).start()

    groups = len(COLUMN_GROUPS)
    pace = (
        ((10, 9), (11, 9), (12, 10), (12, 11)),
        ((13, 12), (13, 12), (14, 13), (15, 13)),
        ((16, 14), (17, 14), (18, 14), (18, 14)),
        ((20, 15),) * 4,
    )
    for group in range(groups):
        weight_group(group)
        project(2, part_o, group)
        x_copy(group, 0).start()
        x_copy(group, 1).start()
        pump_to(*pace[group][0])
        project(1, part_r, group)
        x_copy(group, 2).start()
        pump_to(*pace[group][1])
        project(3, part_l, group)
        x_copy(group, 3).start()
        if group in (1, 2):
            relay(group - 1)
        pump_to(*pace[group][2])
        project(0, part_own, group)
        pump_to(*pace[group][3])
        if group == 2:
            relay(group)
    inner_out[...] = lax.dot_general(
        jnp.ones((8, 128), jnp.float32), inner_acc[...],
        (((1,), (1,)), ((), ())), precision=HIGHEST,
        preferred_element_type=jnp.float32,
    )
    i_copies = [
        remote(inner_out, inner_in.at[d], i_send.at[d], i_recv.at[d], at_x(d))
        for d in range(1, NX)
    ]
    for copy in i_copies:
        copy.start()
    relay(groups - 1)
    for copy in i_copies:
        copy.wait_recv()
    norm_total = jnp.sum(dir_ref[...] * dir_ref[...]) + EPSILON
    level = (inner_out[...] + inner_in[1] + inner_in[2] + inner_in[3]) / norm_total
    level_ref[...] = level[0:1, :]
    level_wide = jnp.transpose(jnp.broadcast_to(level[0:1, :], (128, TOKENS)))
    weight_drain()
    halo.wait_send()
    for copy in y_copies + z_copies + i_copies:
        copy.wait_send()
    for group in range(groups):
        for index in range(2, 6):
            x_copy(group, index).wait_recv()
        for i, e in enumerate(COLUMN_GROUPS[group]):
            start = GROUP_START[group] + i * 128
            cols = slice(start, start + 128)
            summed = (
                part_own[:, cols].astype(jnp.float32)
                + from_l[:, cols].astype(jnp.float32)
                + from_r[:, cols].astype(jnp.float32)
            )
            at = yy(e)
            out_ref[:, pl.ds(pl.multiple_of(at * 128, 128), 128)] = (
                summed - level_wide * dir_ref[pl.ds(x * NY + at, 1), :]
            ).astype(jnp.bfloat16)
    for group in range(groups):
        for index in range(6):
            x_copy(group, index).wait_send()


def shards(q_feat, k_feat, v_feat, short_taps, decay_rate, residue, out_weight, direction):
    f32, bf16 = jnp.float32, jnp.bfloat16
    vmem = pltpu.VMEM
    dma = pltpu.SemaphoreType.DMA
    ablated, level = pl.pallas_call(
        kernel,
        out_shape=(
            jax.ShapeDtypeStruct((TOKENS, WIDTH), bf16),
            jax.ShapeDtypeStruct((1, TOKENS), f32),
        ),
        in_specs=[pl.BlockSpec(memory_space=pltpu.HBM)] * 8,
        out_specs=(pl.BlockSpec(memory_space=pltpu.VMEM),) * 2,
        scratch_shapes=[
            vmem((TOKENS, WIDTH), bf16),
            vmem((TOKENS, WIDTH), bf16),
            vmem((TOKENS, WIDTH), bf16),
            vmem((3, 3, WIDTH), f32),
            vmem((MODES, WIDTH), f32),
            vmem((MODES, WIDTH), f32),
            vmem((32, 128), f32),
            vmem((9 * GROUPS, 128), f32),
            vmem((128, 128), f32),
            vmem((128, 128), f32),
            vmem((GROUPS * PITCH, 128), f32),
            vmem((GROUPS * PITCH, 128), f32),
            vmem((GROUPS * PITCH, 128), f32),
            vmem((TOKENS, GROUPS, 128), f32),
            vmem((TOKENS, GROUPS, 128), f32),
            vmem((TOKENS, GROUPS, 128), f32),
            vmem((GROUPS * PITCH, 128), f32),
            vmem((TOKENS, WIDTH), bf16),
            vmem((128, 128), f32),
            vmem((128, 128), f32),
            vmem((128, 128), f32),
            vmem((8, WIDTH), f32),
            vmem((8, WIDTH), f32),
            vmem((128, 128), bf16),
            vmem((NY, 128, 128), bf16),
            vmem((128, 128), bf16),
            vmem((NZ, 128, 128), bf16),
            vmem((NZ, NY, WIDTH, 128), bf16),
            vmem((TOKENS, WIDTH), bf16),
            vmem((TOKENS, WIDTH), bf16),
            vmem((TOKENS, WIDTH), bf16),
            vmem((TOKENS, WIDTH), bf16),
            vmem((128, WIDTH), bf16),
            vmem((128, WIDTH), bf16),
            vmem((TOKENS, WIDTH), bf16),
            vmem((TOKENS, WIDTH), bf16),
            vmem((TOKENS, 128), f32),
            vmem((8, TOKENS), f32),
            vmem((NX, 8, TOKENS), f32),
            dma((8,)), dma((2,)), dma((NY,)), dma((NY,)), dma((NZ,)), dma((NZ,)),
            dma((62,)), dma((62,)), dma((31,)), dma((31,)),
            dma((24,)), dma((24,)), dma((NX,)), dma((NX,)),
        ],
        compiler_params=pltpu.CompilerParams(
            collective_id=0, has_side_effects=True, vmem_limit_bytes=63 << 20
        ),
        name="mixing",
    )(
        q_feat, k_feat, v_feat, short_taps, decay_rate.T, residue.T, out_weight,
        direction.reshape(32, 128),
    )
    return ablated, level.reshape(TOKENS)


def solution(mesh):
    placed = (
        P(("dp", "ctx"), "tp"),
        P(("dp", "ctx"), "tp"),
        P(("dp", "ctx"), "tp"),
        P(None, None, "tp"),
        P("tp", None),
        P("tp", None),
        P("tp", "ctx"),
        P(),
    )
    return jax.shard_map(
        shards,
        mesh=mesh,
        in_specs=placed,
        out_specs=(P(("dp", "ctx"), "tp"), P(("dp", "ctx"))),
        check_vma=False,
    )
```
